32 devices in a mesh: dp: 4 (over y, core), bucket: 8 (over z, x).
Axes of the slice: x: 2, y: 2, z: 4, core: 2. Of those that a mesh axis runs over, the one named last changes fastest.
Arguments:
- frames: bfloat16 [49152, 512], P(('dp', 'bucket')), may hold values from -60 to 60, as said below
- lengths: int32 [4, 256], P('dp'), may hold values from 1 to 48, as said below
- owners: int32 [4, 256], P('dp'), may hold values from 0 to 7, as said below
- upstream: bfloat16 [24576, 512], P(('dp', 'bucket')), may hold values from -6 to 6
- ln_gain: float32 [512], replicated, may hold values from 0.1 to 1.9
- w_in: bfloat16 [512, 1024], replicated, may hold values from -0.25 to 0.25
- w_dw: float32 [512, 31], replicated, may hold values from -1 to 1
- bn_gain: float32 [512], replicated, may hold values from 0.1 to 1.9
- bn_bias: float32 [512], replicated, may hold values from -3 to 3
- w_out: bfloat16 [512, 512], replicated, may hold values from -0.25 to 0.25
Outputs:
- out_frames: bfloat16 [24576, 512], P(('dp', 'bucket'))
- grad_frames: bfloat16 [49152, 512], P(('dp', 'bucket'))
- grad_w_in: float32 [512, 1024], P('bucket')
- grad_w_out: float32 [512, 512], P('bucket')
- grad_w_dw: float32 [512, 31], P('bucket')
- grad_ln_gain: float32 [512], P('bucket')
- grad_bn_gain: float32 [512], replicated
- grad_bn_bias: float32 [512], replicated
The draws below stay inside these ranges and needn't reach their ends.
Inputs may be any that keep to these rules, and one draw needn't show every extreme that they name: `frames`: frame rows past an utterance's length are not read. In each group every owner receives exactly 4 utterances from each loader shard, their lengths sum to exactly 768 with one of exactly 48, and the lengths an owner receives do not fall with the loader index. `owners`: in each group and loader shard every owner index appears exactly 4 times.
All inputs are finite; a program needn't handle non-finite values.
Results may differ from the reference program's by a relative error of at most 0.013.
Values may be sent and summed in bfloat16 or wider, within the bound.
A program may use at most 128 MiB of HBM per device.

```python
import math
import jax
import jax.numpy as jnp
from jax import lax

D = 512
K = 31
SLOTS = 32
LMAX = 48
GROUPS = 4
LOADERS = 8
PAIR = 4
OWN_ROWS = 768
OWNED_ALL = 24576


def plan_layout(key):
    base_key = jax.random.fold_in(key, 11)
    len_key, perm_key = jax.random.split(base_key)
    cell_count = (SLOTS - 1) * (LMAX - 1)
    deficit = SLOTS * LMAX - OWN_ROWS

    def owner_lengths(sub_key):
        bias_key, noise_key = jax.random.split(sub_key)
        biases = jax.random.randint(bias_key, (SLOTS - 1, 1), 0, 1024)
        noises = jax.random.randint(noise_key, (SLOTS - 1, LMAX - 1), 0, 512)
        scores = ((biases + noises) * cell_count).reshape(-1) + jnp.arange(cell_count, dtype=jnp.int32)
        cell_rank = jnp.argsort(jnp.argsort(scores))
        chosen = (cell_rank < deficit).astype(jnp.int32).reshape(SLOTS - 1, LMAX - 1)
        shorter = LMAX - jnp.sum(chosen, axis=1)
        full_set = jnp.concatenate([jnp.full((1,), LMAX, jnp.int32), shorter.astype(jnp.int32)])
        return jnp.sort(full_set)
    owner_keys = jax.random.split(len_key, GROUPS * LOADERS)
    sorted_lengths = jax.vmap(owner_lengths)(owner_keys).reshape(GROUPS, LOADERS * SLOTS)
    perm_keys = jax.random.split(perm_key, GROUPS * LOADERS)
    entries = jax.vmap(lambda sub_key: jax.random.permutation(sub_key, SLOTS))(perm_keys)
    entries = entries.reshape(GROUPS, LOADERS, SLOTS).astype(jnp.int32)
    owner_of = entries // PAIR
    pair_of = entries % PAIR
    loader_ids = jnp.arange(LOADERS, dtype=jnp.int32)[None, :, None]
    pick_index = (owner_of * SLOTS + loader_ids * PAIR + pair_of).reshape(GROUPS, LOADERS * SLOTS)
    picked = jnp.take_along_axis(sorted_lengths, pick_index, axis=1)
    return (picked.astype(jnp.int32), owner_of.reshape(GROUPS, LOADERS * SLOTS).astype(jnp.int32))


def draw_lengths(key, part):
    return plan_layout(key)[0]


def draw_owners(key, part):
    return plan_layout(key)[1]


def draw_frames(key, part):
    picked, owner_of = plan_layout(key)
    frame_key = jax.random.fold_in(key, 23)
    noise_key, vector_key, row_key = jax.random.split(frame_key, 3)
    row_total = GROUPS * LOADERS * SLOTS * LMAX
    device_rank = jnp.arange(GROUPS, dtype=jnp.int32)[:, None] * LOADERS + owner_of
    ramp_value = device_rank.astype(jnp.float32).reshape(-1) / float(max(GROUPS * LOADERS - 1, 1))
    noise_part = jax.random.normal(noise_key, (row_total, D), jnp.float32)
    row_scale = jnp.exp(jax.random.uniform(row_key, (row_total,), jnp.float32, 0.0, math.log(3.0)))
    amplitude = jnp.exp(ramp_value * math.log(3.0))
    common = jnp.clip(jax.random.normal(vector_key, (D,), jnp.float32), -3.0, 3.0)
    strength = 0.25 * jnp.repeat(amplitude, LMAX) * row_scale
    return (noise_part + strength[:, None] * common[None, :]).astype(jnp.bfloat16)


def levels(own_key, dims, cuts, least, high):
    gain, own = 1.0, jax.random.fold_in(own_key, 6)
    for axis_at, shards_of in cuts:
        heights = jnp.exp(jax.random.uniform(jax.random.fold_in(own, axis_at), (shards_of,), jnp.float32, least / len(cuts), high / len(cuts)))
        gain = gain * jnp.repeat(heights, dims[axis_at] // shards_of).reshape([-1 if axis == axis_at else 1 for axis in range(len(dims))])
    return gain


def noise(own_key, extent, deviation, most, shards=(), kind=jnp.bfloat16):
    values = jax.random.normal(own_key, extent, jnp.float32) * deviation
    if len(shards) > 0:
        values = levels(own_key, extent, shards, -0.22, 0.18) * values
    return jnp.clip(values, min=-most, max=most).astype(kind)


def setup_inputs(seed: int = 0) -> dict:
    seeds = jax.random.split(jax.random.key(seed), 11)
    return {
        "frames": draw_frames(jax.random.fold_in(seeds[10], 71), 0),
        "lengths": draw_lengths(jax.random.fold_in(seeds[10], 71), 0),
        "owners": draw_owners(jax.random.fold_in(seeds[10], 71), 0),
        "upstream": noise(seeds[3], (OWNED_ALL, D), 1.0, 6.0, ((0, 32),)),
        "ln_gain": jnp.clip(1.0 + 0.18 * jax.random.normal(seeds[4], (D,), jnp.float32), 0.1, 1.9),
        "w_in": noise(seeds[5], (D, 2 * D), D ** -0.5, 0.25),
        "w_dw": noise(seeds[6], (D, K), K ** -0.5, 1.0, (), jnp.float32),
        "bn_gain": jnp.clip(1.0 + 0.18 * jax.random.normal(seeds[7], (D,), jnp.float32), 0.1, 1.9),
        "bn_bias": noise(seeds[8], (D,), 0.5, 3.0, (), jnp.float32),
        "w_out": noise(seeds[9], (D, D), D ** -0.5, 0.25),
    }


EPSILON = 1e-05

def normalize_rows(frame_rows, ln_gain):
    values = frame_rows.astype(jnp.float32)
    centred = values - lax.optimization_barrier(jnp.mean(values, axis=1, keepdims=True))
    inverse = lax.rsqrt(lax.optimization_barrier(jnp.mean(centred * centred, axis=1, keepdims=True)) + EPSILON)
    normed = centred * inverse
    return ((normed * ln_gain).astype(jnp.bfloat16), normed, inverse)

def normalize_back(grad_h, normed, inverse, ln_gain):
    scaled = grad_h * ln_gain
    inner_sum = lax.optimization_barrier(jnp.mean(scaled * normed, axis=1, keepdims=True))
    return inverse * (scaled - lax.optimization_barrier(jnp.mean(scaled, axis=1, keepdims=True)) - normed * inner_sum)

def conv_forward(gated_rows, segment, w_dw):
    width_half = w_dw.shape[1] // 2
    length_all = gated_rows.shape[1]
    padded = jnp.pad(gated_rows, ((0, 0), (width_half, width_half), (0, 0)))
    seg_pad = jnp.pad(segment, ((0, 0), (width_half, width_half)), constant_values=-1)
    result = jnp.zeros(gated_rows.shape, jnp.float32)
    for offset in range(w_dw.shape[1]):
        same_seg = (seg_pad[:, offset:offset + length_all] == segment)[:, :, None]
        shifted = padded[:, offset:offset + length_all].astype(jnp.float32)
        result = result + jnp.where(same_seg, shifted, 0.0) * w_dw[:, offset]
    return result

def conv_backward(grad_conv, gated_rows, segment, w_dw):
    width_half = w_dw.shape[1] // 2
    length_all = gated_rows.shape[1]
    padded = jnp.pad(gated_rows, ((0, 0), (width_half, width_half), (0, 0)))
    grad_pad = jnp.pad(grad_conv, ((0, 0), (width_half, width_half), (0, 0)))
    seg_pad = jnp.pad(segment, ((0, 0), (width_half, width_half)), constant_values=-1)
    grad_gated = jnp.zeros(grad_conv.shape, jnp.float32)
    grad_cols = []
    for offset in range(w_dw.shape[1]):
        same_fwd = (seg_pad[:, offset:offset + length_all] == segment)[:, :, None]
        shifted = jnp.where(same_fwd, padded[:, offset:offset + length_all].astype(jnp.float32), 0.0)
        grad_cols.append(lax.optimization_barrier(jnp.sum(shifted * grad_conv, axis=(0, 1))))
        back_start = 2 * width_half - offset
        same_back = (seg_pad[:, back_start:back_start + length_all] == segment)[:, :, None]
        grad_gated = grad_gated + jnp.where(same_back, grad_pad[:, back_start:back_start + length_all], 0.0) * w_dw[:, offset]
    return (grad_gated, jnp.stack(grad_cols, axis=1))

def reference(frames, lengths, owners, upstream, ln_gain, w_in, w_dw, bn_gain, bn_bias, w_out):
    utterances = LOADERS * SLOTS
    frame_groups = frames.reshape(GROUPS, utterances * LMAX, D)
    grad_groups = upstream.reshape(GROUPS, LOADERS * OWN_ROWS, D)
    position = jnp.arange(LMAX, dtype=jnp.int32)
    segment = jnp.broadcast_to(jnp.arange(utterances, dtype=jnp.int32)[:, None], (utterances, LMAX))
    total_frames = float(GROUPS * LOADERS * OWN_ROWS)
    owner_ids = jnp.arange(LOADERS, dtype=jnp.int32)

    def layout(lens_group, dest_group):
        valid_rows = position[None, :] < lens_group[:, None]
        onehot = (dest_group[:, None] == owner_ids[None, :]).astype(jnp.int32)
        weighted = onehot * lens_group[:, None]
        earlier = jnp.cumsum(weighted, axis=0) - weighted
        starts = lax.optimization_barrier(jnp.sum(earlier * onehot, axis=1))
        target = dest_group[:, None] * OWN_ROWS + starts[:, None] + position[None, :]
        target = jnp.where(valid_rows, target, LOADERS * OWN_ROWS)
        return target.reshape(-1).astype(jnp.int32)

    def forward(frame_block, lens_group):
        valid_rows = (position[None, :] < lens_group[:, None]).reshape(-1)
        normed_h, normed, inverse = normalize_rows(frame_block, ln_gain)
        projected = jnp.dot(normed_h, w_in, preferred_element_type=jnp.float32)
        linear = projected[:, :D]
        gate_sig = jax.nn.sigmoid(projected[:, D:])
        gated_rows = jnp.where(valid_rows[:, None], linear * gate_sig, 0.0).astype(jnp.bfloat16)
        conv_rows = conv_forward(gated_rows.reshape(utterances, LMAX, D), segment, w_dw).reshape(-1, D)
        return (valid_rows, normed_h, normed, inverse, linear, gate_sig, gated_rows, conv_rows)

    def moments(inputs_group):
        frame_block, lens_group = inputs_group
        valid_rows = forward(frame_block, lens_group)[0]
        conv_rows = forward(frame_block, lens_group)[7]
        masked = jnp.where(valid_rows[:, None], conv_rows, 0.0)
        return (lax.optimization_barrier(jnp.sum(masked, axis=0)), lax.optimization_barrier(jnp.sum(masked * masked, axis=0)))
    first_parts, second_parts = lax.map(moments, (frame_groups, lengths))
    centre = lax.optimization_barrier(jnp.sum(first_parts, axis=0)) / total_frames
    variance = lax.optimization_barrier(jnp.sum(second_parts, axis=0)) / total_frames - centre * centre
    bn_inverse = lax.rsqrt(variance + EPSILON)

    def batch_part(conv_rows):
        bn_normed = (conv_rows - centre) * bn_inverse
        bn_value = bn_normed * bn_gain + bn_bias
        bn_sig = jax.nn.sigmoid(bn_value)
        swished = (bn_value * bn_sig).astype(jnp.bfloat16)
        return (bn_normed, bn_value, bn_sig, swished)

    def grad_slots(grad_block, valid_rows, target):
        picked = jnp.take(grad_block, jnp.minimum(target, LOADERS * OWN_ROWS - 1), axis=0)
        return jnp.where(valid_rows[:, None], picked, 0.0).astype(jnp.bfloat16)

    def second_pass(inputs_group):
        frame_block, grad_block, lens_group, dest_group = inputs_group
        target = layout(lens_group, dest_group)
        valid_rows, normed_h, normed, inverse, linear, gate_sig, gated_rows, conv_rows = forward(frame_block, lens_group)
        bn_normed, bn_value, bn_sig, swished = batch_part(conv_rows)
        out_rows = jnp.dot(swished, w_out, preferred_element_type=jnp.float32).astype(jnp.bfloat16)
        packed = jnp.zeros((LOADERS * OWN_ROWS, D), jnp.bfloat16).at[target].set(out_rows, mode='drop')
        grad_out = grad_slots(grad_block, valid_rows, target)
        grad_swish = jnp.dot(grad_out, w_out.T, preferred_element_type=jnp.float32)
        grad_bn_rows = grad_swish * (bn_sig * (1.0 + bn_value * (1.0 - bn_sig)))
        return (packed, lax.optimization_barrier(jnp.sum(grad_bn_rows, axis=0)), lax.optimization_barrier(jnp.sum(grad_bn_rows * bn_normed, axis=0)))
    packed_all, bias_parts, gain_parts = lax.map(second_pass, (frame_groups, grad_groups, lengths, owners))
    bias_total = lax.optimization_barrier(jnp.sum(bias_parts, axis=0))
    gain_total = lax.optimization_barrier(jnp.sum(gain_parts, axis=0))

    def third_pass(inputs_group):
        frame_block, grad_block, lens_group, dest_group = inputs_group
        target = layout(lens_group, dest_group)
        valid_rows, normed_h, normed, inverse, linear, gate_sig, gated_rows, conv_rows = forward(frame_block, lens_group)
        bn_normed, bn_value, bn_sig, swished = batch_part(conv_rows)
        grad_out = grad_slots(grad_block, valid_rows, target)
        grad_wout = jnp.dot(swished.T, grad_out, preferred_element_type=jnp.float32)
        grad_swish = jnp.dot(grad_out, w_out.T, preferred_element_type=jnp.float32)
        grad_bn_rows = grad_swish * (bn_sig * (1.0 + bn_value * (1.0 - bn_sig)))
        grad_conv = jnp.where(valid_rows[:, None], bn_gain * bn_inverse * (grad_bn_rows - bias_total / total_frames - bn_normed * (gain_total / total_frames)), 0.0)
        grad_gated, grad_wdw = conv_backward(grad_conv.reshape(utterances, LMAX, D), gated_rows.reshape(utterances, LMAX, D), segment, w_dw)
        grad_gated = jnp.where(valid_rows[:, None], grad_gated.reshape(-1, D), 0.0)
        grad_proj = jnp.concatenate([grad_gated * gate_sig, grad_gated * linear * gate_sig * (1.0 - gate_sig)], axis=1).astype(jnp.bfloat16)
        grad_win = jnp.dot(normed_h.T, grad_proj, preferred_element_type=jnp.float32)
        grad_h = jnp.dot(grad_proj, w_in.T, preferred_element_type=jnp.float32)
        grad_ln = lax.optimization_barrier(jnp.sum(grad_h * normed, axis=0))
        grad_rows = normalize_back(grad_h, normed, inverse, ln_gain)
        grad_rows = jnp.where(valid_rows[:, None], grad_rows, 0.0).astype(jnp.bfloat16)
        return (grad_rows, grad_win, grad_wout, grad_wdw, grad_ln)
    grad_all, win_parts, wout_parts, wdw_parts, ln_parts = lax.map(third_pass, (frame_groups, grad_groups, lengths, owners))
    return (packed_all.reshape(-1, D), grad_all.reshape(-1, D), lax.optimization_barrier(jnp.sum(win_parts, axis=0)), lax.optimization_barrier(jnp.sum(wout_parts, axis=0)), lax.optimization_barrier(jnp.sum(wdw_parts, axis=0)), lax.optimization_barrier(jnp.sum(ln_parts, axis=0)), gain_total, bias_total)
```

```python
import functools

import jax
import jax.numpy as jnp
from jax import lax
from jax.experimental import pallas as pl
from jax.experimental.pallas import tpu as pltpu
from jax.sharding import PartitionSpec as P

EPSILON = 1e-05
LANES = 128
SUB = 8
MESH = pl.DeviceIdType.MESH
VMEM_LIMIT = 48 << 20


def lane(c):
    return slice(c * LANES, (c + 1) * LANES)


def row_of(packed, first, blocks):
    return jnp.concatenate([packed[first + c : first + c + 1] for c in range(blocks)], axis=1)


def live_rows(lens_ref, first, count, span, width):
    position = lax.broadcasted_iota(jnp.int32, (span, width), 0)
    return [position < lens_ref[first + i] for i in range(count)]


def keep_live(values, masks, span):
    parts = [
        jnp.where(masks[i], values[i * span : (i + 1) * span], 0.0) for i in range(len(masks))
    ]
    return jnp.concatenate(parts, axis=0)


def layer_norm(frame_rows):
    values = frame_rows.astype(jnp.float32)
    centred = values - jnp.mean(values, axis=1, keepdims=True)
    inverse = lax.rsqrt(jnp.mean(centred * centred, axis=1, keepdims=True) + EPSILON)
    return centred * inverse, inverse


def project(frame_rows, gain, w_in):
    normed, inverse = layer_norm(frame_rows)
    h = (normed * gain).astype(jnp.bfloat16)
    projected = jnp.dot(h, w_in, preferred_element_type=jnp.float32)
    half = projected.shape[1] // 2
    return normed, inverse, h, projected[:, :half], jax.nn.sigmoid(projected[:, half:])


def shifted_sum(padded, weight, span, taps):
    total = None
    for residue in range(SUB):
        part = None
        for k in range(residue, taps + 1, SUB):
            if k == 0:
                continue
            term = padded[k - residue : k - residue + span + SUB] * weight(k)
            part = term if part is None else part + term
        if residue:
            part = pltpu.roll(part, span + SUB - residue, 0)
        part = part[:span]
        total = part if total is None else total + part
    return total


def forward_kernel(group, span, taps, lens_ref, frames_ref, gain_ref, w_in_ref, w_dw_ref,
                   conv_ref, sums_ref, padded):
    step = pl.program_id(0)
    blocks = conv_ref.shape[1] // LANES
    edge = (padded.shape[2] - span) // 2

    @pl.when(step == 0)
    def _():
        padded[...] = jnp.zeros_like(padded)
        sums_ref[...] = jnp.zeros_like(sums_ref)

    masks = live_rows(lens_ref, step * group, group, span, conv_ref.shape[1])
    _, _, _, linear, gate = project(frames_ref[...], gain_ref[...], w_in_ref[...])
    gated = keep_live(linear * gate, masks, span).astype(jnp.bfloat16).astype(jnp.float32)
    for u in range(group):
        for c in range(blocks):
            padded[u, c, edge : edge + span] = gated[u * span : (u + 1) * span, lane(c)]

    def one(u, carry):
        live = lax.broadcasted_iota(jnp.int32, (span, LANES), 0) < lens_ref[step * group + u]
        start = pl.multiple_of(u * span, SUB)
        for c in range(blocks):
            conv = shifted_sum(
                padded[u, c], lambda k: w_dw_ref[k - 1 : k, lane(c)], span, taps
            )
            conv_ref[pl.ds(start, span), lane(c)] = conv
            masked = jnp.where(live, conv, 0.0)
            sums_ref[c : c + 1] += jnp.sum(masked, axis=0, keepdims=True)
            sums_ref[blocks + c : blocks + c + 1] += jnp.sum(
                masked * masked, axis=0, keepdims=True
            )
        return carry

    lax.fori_loop(0, group, one, 0)


def batch_norm(total_ref, conv, total_frames, blocks):
    packed = total_ref[...]
    centre = row_of(packed, 0, blocks) / total_frames
    variance = row_of(packed, blocks, blocks) / total_frames - centre * centre
    inverse = lax.rsqrt(variance + EPSILON)
    return (conv - centre) * inverse, inverse


def middle_kernel(group, span, total_frames, lens_ref, conv_ref, dy_ref, total_ref, bn_gain_ref,
                  bn_bias_ref, w_out_ref, out_ref, grad_bn_ref, sums_ref, grad_wout_ref):
    step = pl.program_id(0)
    width = conv_ref.shape[1]
    blocks = width // LANES

    @pl.when(step == 0)
    def _():
        sums_ref[...] = jnp.zeros_like(sums_ref)
        grad_wout_ref[...] = jnp.zeros_like(grad_wout_ref)

    masks = live_rows(lens_ref, step * group, group, span, width)
    dy = keep_live(dy_ref[...].astype(jnp.float32), masks, span).astype(jnp.bfloat16)
    w_out = w_out_ref[...]
    bn_normed, _ = batch_norm(total_ref, conv_ref[...], total_frames, blocks)
    bn = bn_normed * bn_gain_ref[...] + bn_bias_ref[...]
    sig = jax.nn.sigmoid(bn)
    swished = (bn * sig).astype(jnp.bfloat16)
    out_ref[...] = jnp.dot(swished, w_out, preferred_element_type=jnp.float32).astype(jnp.bfloat16)
    grad_wout_ref[...] += lax.dot_general(
        swished, dy, (((0,), (0,)), ((), ())), preferred_element_type=jnp.float32
    )
    grad_swish = lax.dot_general(
        dy, w_out, (((1,), (1,)), ((), ())), preferred_element_type=jnp.float32
    )
    grad_bn = grad_swish * (sig * (1.0 + bn * (1.0 - sig)))
    grad_bn_ref[...] = grad_bn
    bias_row = jnp.sum(grad_bn, axis=0, keepdims=True)
    gain_row = jnp.sum(grad_bn * bn_normed, axis=0, keepdims=True)
    for c in range(blocks):
        sums_ref[c : c + 1] += bias_row[:, lane(c)]
        sums_ref[blocks + c : blocks + c + 1] += gain_row[:, lane(c)]


def backward_kernel(group, span, taps, total_frames, lens_ref, frames_ref, conv_ref, grad_bn_ref,
                    total_ref, back_ref, gain_ref, bn_gain_ref, w_in_ref, w_dw_ref, wout_ref,
                    grad_frames_ref, packed_ref, padded, grad_pad, gated_grad, w_acc, win_acc,
                    ln_acc, flat):
    step = pl.program_id(0)
    width = conv_ref.shape[1]
    blocks = width // LANES
    edge = (padded.shape[2] - span) // 2

    @pl.when(step == 0)
    def _():
        padded[...] = jnp.zeros_like(padded)
        grad_pad[...] = jnp.zeros_like(grad_pad)
        w_acc[...] = jnp.zeros_like(w_acc)
        win_acc[...] = jnp.zeros_like(win_acc)
        ln_acc[...] = jnp.zeros_like(ln_acc)

    masks = live_rows(lens_ref, step * group, group, span, width)
    w_in = w_in_ref[...]
    normed, inverse, h, linear, gate = project(frames_ref[...], gain_ref[...], w_in)
    gated = keep_live(linear * gate, masks, span).astype(jnp.bfloat16).astype(jnp.float32)
    bn_normed, bn_inverse = batch_norm(total_ref, conv_ref[...], total_frames, blocks)
    back = back_ref[...]
    bias_mean = row_of(back, 0, blocks) / total_frames
    gain_mean = row_of(back, blocks, blocks) / total_frames
    grad_conv = keep_live(
        bn_gain_ref[...] * bn_inverse * (grad_bn_ref[...] - bias_mean - bn_normed * gain_mean),
        masks,
        span,
    )
    for u in range(group):
        for c in range(blocks):
            rows = slice(u * span, (u + 1) * span)
            padded[u, c, edge : edge + span] = gated[rows, lane(c)]
            grad_pad[u, c, edge : edge + span] = grad_conv[rows, lane(c)]

    def one(u, carry):
        start = pl.multiple_of(u * span, SUB)
        for c in range(blocks):
            grads = grad_pad[u, c]
            gated_grad[pl.ds(start, span), lane(c)] = shifted_sum(
                grads, lambda k: w_dw_ref[taps - k : taps - k + 1, lane(c)], span, taps
            )
            inner = grads[edge - SUB : edge + span + SUB]
            frame = padded[u, c]
            for residue in range(SUB):
                moved = inner if residue == 0 else pltpu.roll(inner, residue, 0)
                moved = moved[SUB:]
                for k in range(residue, taps + 1, SUB):
                    if k == 0:
                        continue
                    term = moved * frame[k - residue : k - residue + span + SUB]
                    part = term[:SUB]
                    for i in range(1, span // SUB + 1):
                        part = part + term[i * SUB : (i + 1) * SUB]
                    w_acc[c, k - 1] += part
        return carry

    lax.fori_loop(0, group, one, 0)

    grad_gated = keep_live(gated_grad[...], masks, span)
    left = grad_gated * gate
    grad_a = jnp.concatenate(
        [left.astype(jnp.bfloat16), (left * linear * (1.0 - gate)).astype(jnp.bfloat16)], axis=1
    )
    win_acc[...] += lax.dot_general(
        h, grad_a, (((0,), (0,)), ((), ())), preferred_element_type=jnp.float32
    )
    grad_h = lax.dot_general(
        grad_a, w_in, (((1,), (1,)), ((), ())), preferred_element_type=jnp.float32
    )
    ln_acc[...] += jnp.sum(grad_h * normed, axis=0, keepdims=True)
    scaled = grad_h * gain_ref[...]
    inner_mean = jnp.mean(scaled * normed, axis=1, keepdims=True)
    grad_x = inverse * (scaled - jnp.mean(scaled, axis=1, keepdims=True) - normed * inner_mean)
    grad_frames_ref[...] = keep_live(grad_x, masks, span).astype(jnp.bfloat16)

    @pl.when(step == pl.num_programs(0) - 1)
    def _():
        owners = packed_ref.shape[0]
        share = width // owners
        wide = w_in.shape[1] // LANES
        for c in range(blocks):
            flat[...] = jnp.zeros_like(flat)
            for k in range(taps):
                flat[k : k + 1] = jnp.sum(w_acc[c, k], axis=0, keepdims=True)
            flat[taps : taps + 1] = ln_acc[:, lane(c)]
            turned = flat[...].T.astype(jnp.bfloat16)
            for i in range(LANES // share):
                packed_ref[c * (LANES // share) + i, (wide + blocks) * share :] = turned[
                    i * share : (i + 1) * share
                ]
        for j in range(owners):
            rows = slice(j * share, (j + 1) * share)
            for c in range(wide):
                packed_ref[j, c * share : (c + 1) * share] = win_acc[rows, lane(c)].astype(
                    jnp.bfloat16
                )
            for c in range(blocks):
                packed_ref[j, (wide + c) * share : (wide + c + 1) * share] = wout_ref[
                    rows, lane(c)
                ].astype(jnp.bfloat16)


def whole(shape):
    return pl.BlockSpec(shape, lambda i, *_: (0,) * len(shape))


def sum_kernel(groups, owners, part_ref, out_ref, slots, send_sems, recv_sems):
    count = groups * owners
    me = lax.axis_index("dp") * owners + lax.axis_index("bucket")
    barrier = pltpu.get_barrier_semaphore()

    def peer_of(i):
        other = lax.rem(me + i, count)
        return (other // owners, lax.rem(other, owners))

    def greet(i, carry):
        pl.semaphore_signal(barrier, inc=1, device_id=peer_of(i), device_id_type=MESH)
        return carry

    lax.fori_loop(1, count, greet, 0)
    pl.semaphore_wait(barrier, count - 1)

    def copy_to(i):
        return pltpu.make_async_remote_copy(
            src_ref=part_ref,
            dst_ref=slots.at[me],
            send_sem=send_sems.at[i],
            recv_sem=recv_sems.at[me],
            device_id=peer_of(i),
            device_id_type=MESH,
        )

    def send(i, carry):
        copy_to(i).start()
        return carry

    lax.fori_loop(1, count, send, 0)
    slots[me] = part_ref[...]

    def receive(i, carry):
        source = lax.rem(me + i, count)
        pltpu.make_async_remote_copy(
            src_ref=part_ref,
            dst_ref=slots.at[source],
            send_sem=send_sems.at[i],
            recv_sem=recv_sems.at[source],
            device_id=peer_of(i),
            device_id_type=MESH,
        ).wait_recv()
        return carry

    lax.fori_loop(1, count, receive, 0)
    out_ref[...] = lax.fori_loop(
        1, count, lambda i, total: total + slots[i], slots[0]
    )

    def sent(i, carry):
        copy_to(i).wait_send()
        return carry

    lax.fori_loop(1, count, sent, 0)


def sum_everywhere(part, collective_id):
    groups, owners = lax.axis_size("dp"), lax.axis_size("bucket")
    count = groups * owners
    return pl.pallas_call(
        functools.partial(sum_kernel, groups, owners),
        out_shape=jax.ShapeDtypeStruct(part.shape, part.dtype),
        in_specs=[pl.BlockSpec(memory_space=pltpu.VMEM)],
        out_specs=pl.BlockSpec(memory_space=pltpu.VMEM),
        scratch_shapes=[
            pltpu.VMEM((count,) + part.shape, part.dtype),
            pltpu.SemaphoreType.DMA((count,)),
            pltpu.SemaphoreType.DMA((count,)),
        ],
        compiler_params=pltpu.CompilerParams(collective_id=collective_id, has_side_effects=True),
        cost_estimate=pl.CostEstimate(flops=10**6, bytes_accessed=2 * 10**7, transcendentals=0),
        name="sum_everywhere_%d" % collective_id,
    )(part)


def reduce_kernel(groups, owners, src, out, first, first_sum, second, second_sum, third, mine,
                  core_sems, pair_sems, row_sems, all_sems):
    dp, me = lax.axis_index("dp"), lax.axis_index("bucket")
    halves = groups // 2
    core, side = lax.rem(dp, 2), dp // 2
    chunk = core * halves + side
    partner = side * 2 + (1 - core)
    barrier = pltpu.get_barrier_semaphore()

    def group_peer(i):
        return lax.rem(dp + i, groups)

    def owner_peer(i):
        return lax.rem(me + i, owners)

    def greet_group(i, carry):
        pl.semaphore_signal(barrier, inc=1, device_id=(group_peer(i), me), device_id_type=MESH)
        return carry

    def greet_owner(i, carry):
        pl.semaphore_signal(barrier, inc=1, device_id=(dp, owner_peer(i)), device_id_type=MESH)
        return carry

    lax.fori_loop(1, groups, greet_group, 0)
    lax.fori_loop(1, owners, greet_owner, 0)
    pl.semaphore_wait(barrier, groups + owners - 2)

    def remote(source, target, sems, i, j, device):
        return pltpu.make_async_remote_copy(
            src_ref=source,
            dst_ref=target,
            send_sem=sems.at[0, i],
            recv_sem=sems.at[1, j],
            device_id=device,
            device_id_type=MESH,
        )

    swap = remote(src.at[1 - core], first, core_sems, 0, 0, (partner, me))
    swap.start()
    swap.wait()

    def add_first(j, carry):
        total = src[core, j].astype(jnp.float32) + first[j].astype(jnp.float32)
        first_sum[j] = total.astype(jnp.bfloat16)
        return carry

    lax.fori_loop(0, halves * owners, add_first, 0)

    def to_side(i, arriving):
        other = lax.rem(side + i, halves)
        slot = other if arriving else side
        return remote(
            first_sum.at[pl.ds(other * owners, owners)],
            second.at[slot],
            pair_sems, i, slot,
            (other * 2 + core, me),
        )

    for i in range(1, halves):
        to_side(i, False).start()
    for i in range(1, halves):
        to_side(i, True).wait_recv()

    def add_second(j, carry):
        total = first_sum[side * owners + j].astype(jnp.float32)
        for i in range(1, halves):
            total = total + second[lax.rem(side + i, halves), j].astype(jnp.float32)
        second_sum[j] = total.astype(jnp.bfloat16)
        return carry

    lax.fori_loop(0, owners, add_second, 0)

    def to_owner(i, arriving):
        other = owner_peer(i)
        slot = other if arriving else me
        return remote(second_sum.at[other], third.at[slot], row_sems, i, slot, (dp, other))

    def send_owner(i, carry):
        to_owner(i, False).start()
        return carry

    def wait_owner(i, carry):
        to_owner(i, True).wait_recv()
        return carry

    lax.fori_loop(1, owners, send_owner, 0)
    lax.fori_loop(1, owners, wait_owner, 0)
    third[me] = second_sum[me]
    total = lax.fori_loop(
        1, owners, lambda i, t: t + third[i].astype(jnp.float32), third[0].astype(jnp.float32)
    )
    mine[...] = total.astype(jnp.bfloat16)

    def to_group(i, arriving):
        other = group_peer(i)
        device = other if arriving else dp
        slot = lax.rem(device, 2) * halves + device // 2
        return remote(mine, out.at[slot], all_sems, i, slot, (other, me))

    def send_group(i, carry):
        to_group(i, False).start()
        return carry

    def wait_group(i, carry):
        to_group(i, True).wait_recv()
        return carry

    lax.fori_loop(1, groups, send_group, 0)
    out[chunk] = mine[...]
    lax.fori_loop(1, groups, wait_group, 0)

    def sent_owner(i, carry):
        to_owner(i, False).wait_send()
        return carry

    def sent_group(i, carry):
        to_group(i, False).wait_send()
        return carry

    for i in range(1, halves):
        to_side(i, False).wait_send()
    lax.fori_loop(1, owners, sent_owner, 0)
    lax.fori_loop(1, groups, sent_group, 0)


def reduce_rows(packed, collective_id):
    groups, owners = lax.axis_size("dp"), lax.axis_size("bucket")
    halves = groups // 2
    rows = packed.shape[1] // groups
    source = packed.reshape(owners, 2, halves, rows, LANES).transpose(1, 2, 0, 3, 4)
    source = source.reshape(2, halves * owners, rows, LANES)
    kind = jnp.bfloat16
    return pl.pallas_call(
        functools.partial(reduce_kernel, groups, owners),
        out_shape=jax.ShapeDtypeStruct((groups, rows, LANES), kind),
        in_specs=[pl.BlockSpec(memory_space=pltpu.VMEM)],
        out_specs=pl.BlockSpec(memory_space=pltpu.VMEM),
        scratch_shapes=[
            pltpu.VMEM((halves * owners, rows, LANES), kind),
            pltpu.VMEM((halves * owners, rows, LANES), kind),
            pltpu.VMEM((halves, owners, rows, LANES), kind),
            pltpu.VMEM((owners, rows, LANES), kind),
            pltpu.VMEM((owners, rows, LANES), kind),
            pltpu.VMEM((rows, LANES), kind),
            pltpu.SemaphoreType.DMA((2, 1)),
            pltpu.SemaphoreType.DMA((2, halves)),
            pltpu.SemaphoreType.DMA((2, owners)),
            pltpu.SemaphoreType.DMA((2, groups)),
        ],
        compiler_params=pltpu.CompilerParams(collective_id=collective_id, has_side_effects=True),
        cost_estimate=pl.CostEstimate(flops=10**7, bytes_accessed=6 * 10**7, transcendentals=0),
        name="reduce_rows",
    )(source)


def pick(array, index):
    return array.at[index].get(mode="promise_in_bounds")


def local(frames, lengths, owners, upstream, ln_gain, w_in, w_dw, bn_gain, bn_bias, w_out):
    loaders = lax.axis_size("bucket")
    own_index = lax.axis_index("bucket")
    width = frames.shape[1]
    taps = w_dw.shape[1]
    slot_count = lengths.shape[1] // loaders
    span = frames.shape[0] // slot_count
    pair_count = slot_count // loaders
    own_rows = upstream.shape[0]
    blocks = width // LANES
    total_frames = float(own_rows * loaders * lax.axis_size("dp"))
    lens_all = lengths[0].reshape(loaders, slot_count)
    dest_all = owners[0].reshape(loaders, slot_count)
    owner_ids = jnp.arange(loaders, dtype=jnp.int32)
    onehot = (dest_all[:, :, None] == owner_ids[None, None, :]).astype(jnp.int32)
    earlier = jnp.cumsum(onehot, axis=1) - onehot
    ranking = jnp.sum(earlier * onehot, axis=2)
    send_pos = dest_all * pair_count + ranking
    my_pos = lax.dynamic_index_in_dim(send_pos, own_index, 0, keepdims=False)
    my_lens = lax.dynamic_index_in_dim(lens_all, own_index, 0, keepdims=False)
    slot_ids = jnp.arange(slot_count, dtype=jnp.int32)
    send_order = jnp.sum(
        jnp.where(my_pos[None, :] == slot_ids[:, None], slot_ids[None, :], 0), axis=1
    )
    pair_ids = jnp.arange(pair_count, dtype=jnp.int32)
    to_me = (dest_all == own_index)[:, :, None] & (ranking[:, :, None] == pair_ids[None, None, :])
    recv_lens = jnp.sum(jnp.where(to_me, lens_all[:, :, None], 0), axis=1).reshape(-1)
    starts = jnp.cumsum(recv_lens) - recv_lens
    position = jnp.arange(span, dtype=jnp.int32)
    row_ids = jnp.arange(own_rows, dtype=jnp.int32)
    reached = (starts[None, :] <= row_ids[:, None]).astype(jnp.int32)
    row_slot = jnp.sum(reached, axis=1) - 1
    row_start = jnp.max(reached * starts[None, :], axis=1)
    packed_source = row_slot * span + row_ids - row_start
    slot_target = jnp.minimum(starts[:, None] + position[None, :], own_rows - 1).reshape(-1)

    outgoing = pick(upstream, slot_target).reshape(loaders, pair_count, span, width)
    incoming = lax.all_to_all(outgoing, "bucket", split_axis=0, concat_axis=0, tiled=True)

    group = 4
    steps = slot_count // group
    rows = group * span
    edge = (taps + 1) // 2
    row_block = pl.BlockSpec((rows, width), lambda i, *_: (i, 0))
    all_rows = slot_count * span
    gain_row, bn_gain_row, bn_bias_row = ln_gain[None], bn_gain[None], bn_bias[None]
    w_taps = jnp.pad(w_dw.T, ((0, 1), (0, 0)))
    sums_shape = (2 * blocks, LANES)
    params = pltpu.CompilerParams(
        dimension_semantics=("arbitrary",), vmem_limit_bytes=VMEM_LIMIT
    )
    padded_shape = pltpu.VMEM((group, blocks, span + 2 * edge, LANES), jnp.float32)

    conv, part = pl.pallas_call(
        functools.partial(forward_kernel, group, span, taps),
        grid_spec=pltpu.PrefetchScalarGridSpec(
            num_scalar_prefetch=1,
            grid=(steps,),
            in_specs=[row_block, whole((1, width)), whole(w_in.shape), whole(w_taps.shape)],
            out_specs=[row_block, whole(sums_shape)],
            scratch_shapes=[padded_shape],
        ),
        out_shape=[
            jax.ShapeDtypeStruct((all_rows, width), jnp.float32),
            jax.ShapeDtypeStruct(sums_shape, jnp.float32),
        ],
        compiler_params=params,
        cost_estimate=pl.CostEstimate(
            flops=2 * 10**9, bytes_accessed=4 * 10**7, transcendentals=0
        ),
        name="forward",
    )(my_lens, frames, gain_row, w_in, w_taps)
    totals = sum_everywhere(part, 0)

    work_grad = pick(incoming.reshape(slot_count, span, width), my_pos).reshape(all_rows, width)
    out_rows, grad_bn, back_part, grad_wout = pl.pallas_call(
        functools.partial(middle_kernel, group, span, total_frames),
        grid_spec=pltpu.PrefetchScalarGridSpec(
            num_scalar_prefetch=1,
            grid=(steps,),
            in_specs=[
                row_block, row_block, whole(sums_shape), whole((1, width)), whole((1, width)),
                whole(w_out.shape),
            ],
            out_specs=[row_block, row_block, whole(sums_shape), whole(w_out.shape)],
        ),
        out_shape=[
            jax.ShapeDtypeStruct((all_rows, width), jnp.bfloat16),
            jax.ShapeDtypeStruct((all_rows, width), jnp.float32),
            jax.ShapeDtypeStruct(sums_shape, jnp.float32),
            jax.ShapeDtypeStruct(w_out.shape, jnp.float32),
        ],
        compiler_params=params,
        cost_estimate=pl.CostEstimate(
            flops=3 * 10**9, bytes_accessed=2 * 10**7, transcendentals=0
        ),
        name="middle",
    )(my_lens, conv, work_grad, totals, bn_gain_row, bn_bias_row, w_out)

    leaving = pick(out_rows.reshape(slot_count, span, width), send_order).reshape(
        loaders, pair_count, span, width
    )
    arrived = lax.all_to_all(leaving, "bucket", split_axis=0, concat_axis=0, tiled=True)
    back_totals = sum_everywhere(back_part, 1)

    share = width // loaders
    packed_rows = (w_in.shape[1] // LANES + blocks + 1) * share
    grad_frames, packed = pl.pallas_call(
        functools.partial(backward_kernel, group, span, taps, total_frames),
        grid_spec=pltpu.PrefetchScalarGridSpec(
            num_scalar_prefetch=1,
            grid=(steps,),
            in_specs=[
                row_block, row_block, row_block, whole(sums_shape), whole(sums_shape),
                whole((1, width)), whole((1, width)), whole(w_in.shape), whole(w_taps.shape),
                whole(w_out.shape),
            ],
            out_specs=[row_block, whole((loaders, packed_rows, LANES))],
            scratch_shapes=[
                padded_shape,
                padded_shape,
                pltpu.VMEM((rows, width), jnp.float32),
                pltpu.VMEM((blocks, taps + 1, SUB, LANES), jnp.float32),
                pltpu.VMEM(w_in.shape, jnp.float32),
                pltpu.VMEM((1, width), jnp.float32),
                pltpu.VMEM((LANES, LANES), jnp.float32),
            ],
        ),
        out_shape=[
            jax.ShapeDtypeStruct((all_rows, width), jnp.bfloat16),
            jax.ShapeDtypeStruct((loaders, packed_rows, LANES), jnp.bfloat16),
        ],
        compiler_params=params,
        cost_estimate=pl.CostEstimate(
            flops=6 * 10**9, bytes_accessed=8 * 10**7, transcendentals=0
        ),
        name="backward",
    )(
        my_lens, frames, conv, grad_bn, totals, back_totals, gain_row, bn_gain_row, w_in, w_taps,
        grad_wout,
    )
    reduced = reduce_rows(packed, 2).reshape(-1, share, LANES).astype(jnp.float32)
    out_frames = pick(arrived.reshape(slot_count * span, width), packed_source)
    wide = w_in.shape[1] // LANES
    grad_win = reduced[:wide].transpose(1, 0, 2).reshape(share, -1)
    grad_wo = reduced[wide : wide + blocks].transpose(1, 0, 2).reshape(share, -1)
    last = reduced[wide + blocks]
    flat_back = back_totals.reshape(2, width)
    return (
        out_frames,
        grad_frames,
        grad_win,
        grad_wo,
        last[:, :taps],
        last[:, taps],
        flat_back[1],
        flat_back[0],
    )


def solution(mesh):
    placed = (
        P(("dp", "bucket"), None),
        P("dp", None),
        P("dp", None),
        P(("dp", "bucket"), None),
        P(),
        P(),
        P(),
        P(),
        P(),
        P(),
    )
    return jax.shard_map(
        local,
        mesh=mesh,
        in_specs=placed,
        out_specs=(
            P(("dp", "bucket"), None),
            P(("dp", "bucket"), None),
            P("bucket", None),
            P("bucket", None),
            P("bucket", None),
            P("bucket"),
            P(),
            P(),
        ),
        check_vma=False,
    )
```

```python
import functools

import jax
import jax.numpy as jnp
from jax import lax
from jax.experimental import pallas as pl
from jax.experimental.pallas import tpu as pltpu
from jax.sharding import PartitionSpec as P

EPSILON = 1e-05
LANES = 128
SUB = 8
MESH = pl.DeviceIdType.MESH
VMEM_LIMIT = 48 << 20


def lane(c):
    return slice(c * LANES, (c + 1) * LANES)


def row_of(packed, first, blocks):
    return jnp.concatenate([packed[first + c : first + c + 1] for c in range(blocks)], axis=1)


def live_rows(lens_ref, first, count, span, width):
    position = lax.broadcasted_iota(jnp.int32, (span, width), 0)
    return [position < lens_ref[0, first + i] for i in range(count)]


def keep_live(values, masks, span):
    parts = [
        jnp.where(masks[i], values[i * span : (i + 1) * span], 0.0) for i in range(len(masks))
    ]
    return jnp.concatenate(parts, axis=0)


def layer_norm(frame_rows):
    values = frame_rows.astype(jnp.float32)
    centred = values - jnp.mean(values, axis=1, keepdims=True)
    inverse = lax.rsqrt(jnp.mean(centred * centred, axis=1, keepdims=True) + EPSILON)
    return centred * inverse, inverse


def project(frame_rows, gain, w_in):
    normed, inverse = layer_norm(frame_rows)
    h = (normed * gain).astype(jnp.bfloat16)
    projected = jnp.dot(h, w_in, preferred_element_type=jnp.float32)
    half = projected.shape[1] // 2
    return normed, inverse, h, projected[:, :half], jax.nn.sigmoid(projected[:, half:])


def shifted_sum(padded, weight, span, taps):
    total = None
    for residue in range(SUB):
        part = None
        for k in range(residue, taps + 1, SUB):
            if k == 0:
                continue
            term = padded[k - residue : k - residue + span + SUB] * weight(k)
            part = term if part is None else part + term
        if residue:
            part = pltpu.roll(part, span + SUB - residue, 0)
        part = part[:span]
        total = part if total is None else total + part
    return total


def forward_kernel(group, span, taps, lens_ref, frames_ref, gain_ref, w_in_ref, w_dw_ref,
                   conv_ref, sums_ref, padded):
    step = pl.program_id(0)
    blocks = conv_ref.shape[1] // LANES
    edge = (padded.shape[2] - span) // 2

    @pl.when(step == 0)
    def _():
        padded[...] = jnp.zeros_like(padded)
        sums_ref[...] = jnp.zeros_like(sums_ref)

    masks = live_rows(lens_ref, step * group, group, span, conv_ref.shape[1])
    _, _, _, linear, gate = project(frames_ref[...], gain_ref[...], w_in_ref[...])
    gated = keep_live(linear * gate, masks, span).astype(jnp.bfloat16).astype(jnp.float32)
    for u in range(group):
        for c in range(blocks):
            padded[u, c, edge : edge + span] = gated[u * span : (u + 1) * span, lane(c)]

    def one(u, carry):
        live = lax.broadcasted_iota(jnp.int32, (span, LANES), 0) < lens_ref[0, step * group + u]
        start = pl.multiple_of(u * span, SUB)
        for c in range(blocks):
            conv = shifted_sum(
                padded[u, c], lambda k: w_dw_ref[k - 1 : k, lane(c)], span, taps
            )
            conv_ref[pl.ds(start, span), lane(c)] = conv
            masked = jnp.where(live, conv, 0.0)
            sums_ref[c : c + 1] += jnp.sum(masked, axis=0, keepdims=True)
            sums_ref[blocks + c : blocks + c + 1] += jnp.sum(
                masked * masked, axis=0, keepdims=True
            )
        return carry

    lax.fori_loop(0, group, one, 0)


def batch_norm(total_ref, conv, total_frames, blocks):
    packed = total_ref[...]
    centre = row_of(packed, 0, blocks) / total_frames
    variance = row_of(packed, blocks, blocks) / total_frames - centre * centre
    inverse = lax.rsqrt(variance + EPSILON)
    return (conv - centre) * inverse, inverse


def middle_kernel(group, span, total_frames, lens_ref, conv_ref, dy_ref, total_ref, bn_gain_ref,
                  bn_bias_ref, w_out_ref, out_ref, grad_bn_ref, sums_ref, grad_wout_ref):
    step = pl.program_id(0)
    width = conv_ref.shape[1]
    blocks = width // LANES

    @pl.when(step == 0)
    def _():
        sums_ref[...] = jnp.zeros_like(sums_ref)
        grad_wout_ref[...] = jnp.zeros_like(grad_wout_ref)

    masks = live_rows(lens_ref, step * group, group, span, width)
    slots = [lens_ref[1, step * group + i] for i in range(group)]
    arrived = jnp.concatenate([dy_ref[slot] for slot in slots], axis=0)
    dy = keep_live(arrived.astype(jnp.float32), masks, span).astype(jnp.bfloat16)
    w_out = w_out_ref[...]
    bn_normed, _ = batch_norm(total_ref, conv_ref[...], total_frames, blocks)
    bn = bn_normed * bn_gain_ref[...] + bn_bias_ref[...]
    sig = jax.nn.sigmoid(bn)
    swished = (bn * sig).astype(jnp.bfloat16)
    out = jnp.dot(swished, w_out, preferred_element_type=jnp.float32).astype(jnp.bfloat16)
    for i in range(group):
        out_ref[slots[i]] = out[i * span : (i + 1) * span]
    grad_wout_ref[...] += lax.dot_general(
        swished, dy, (((0,), (0,)), ((), ())), preferred_element_type=jnp.float32
    )
    grad_swish = lax.dot_general(
        dy, w_out, (((1,), (1,)), ((), ())), preferred_element_type=jnp.float32
    )
    grad_bn = grad_swish * (sig * (1.0 + bn * (1.0 - sig)))
    grad_bn_ref[...] = grad_bn
    bias_row = jnp.sum(grad_bn, axis=0, keepdims=True)
    gain_row = jnp.sum(grad_bn * bn_normed, axis=0, keepdims=True)
    for c in range(blocks):
        sums_ref[c : c + 1] += bias_row[:, lane(c)]
        sums_ref[blocks + c : blocks + c + 1] += gain_row[:, lane(c)]


def backward_kernel(group, span, taps, total_frames, lens_ref, frames_ref, conv_ref, grad_bn_ref,
                    total_ref, back_ref, gain_ref, bn_gain_ref, w_in_ref, w_dw_ref, wout_ref,
                    grad_frames_ref, packed_ref, padded, grad_pad, gated_grad, w_acc, win_acc,
                    ln_acc, flat):
    step = pl.program_id(0)
    width = conv_ref.shape[1]
    blocks = width // LANES
    edge = (padded.shape[2] - span) // 2

    @pl.when(step == 0)
    def _():
        padded[...] = jnp.zeros_like(padded)
        grad_pad[...] = jnp.zeros_like(grad_pad)
        w_acc[...] = jnp.zeros_like(w_acc)
        win_acc[...] = jnp.zeros_like(win_acc)
        ln_acc[...] = jnp.zeros_like(ln_acc)

    masks = live_rows(lens_ref, step * group, group, span, width)
    w_in = w_in_ref[...]
    normed, inverse, h, linear, gate = project(frames_ref[...], gain_ref[...], w_in)
    gated = keep_live(linear * gate, masks, span).astype(jnp.bfloat16).astype(jnp.float32)
    bn_normed, bn_inverse = batch_norm(total_ref, conv_ref[...], total_frames, blocks)
    back = back_ref[...]
    bias_mean = row_of(back, 0, blocks) / total_frames
    gain_mean = row_of(back, blocks, blocks) / total_frames
    grad_conv = keep_live(
        bn_gain_ref[...] * bn_inverse * (grad_bn_ref[...] - bias_mean - bn_normed * gain_mean),
        masks,
        span,
    )
    for u in range(group):
        for c in range(blocks):
            rows = slice(u * span, (u + 1) * span)
            padded[u, c, edge : edge + span] = gated[rows, lane(c)]
            grad_pad[u, c, edge : edge + span] = grad_conv[rows, lane(c)]

    def one(u, carry):
        start = pl.multiple_of(u * span, SUB)
        for c in range(blocks):
            grads = grad_pad[u, c]
            gated_grad[pl.ds(start, span), lane(c)] = shifted_sum(
                grads, lambda k: w_dw_ref[taps - k : taps - k + 1, lane(c)], span, taps
            )
            inner = grads[edge - SUB : edge + span + SUB]
            frame = padded[u, c]
            for residue in range(SUB):
                moved = inner if residue == 0 else pltpu.roll(inner, residue, 0)
                moved = moved[SUB:]
                for k in range(residue, taps + 1, SUB):
                    if k == 0:
                        continue
                    term = moved * frame[k - residue : k - residue + span + SUB]
                    part = term[:SUB]
                    for i in range(1, span // SUB + 1):
                        part = part + term[i * SUB : (i + 1) * SUB]
                    w_acc[c, k - 1] += part
        return carry

    lax.fori_loop(0, group, one, 0)

    grad_gated = keep_live(gated_grad[...], masks, span)
    left = grad_gated * gate
    grad_a = jnp.concatenate(
        [left.astype(jnp.bfloat16), (left * linear * (1.0 - gate)).astype(jnp.bfloat16)], axis=1
    )
    win_acc[...] += lax.dot_general(
        h, grad_a, (((0,), (0,)), ((), ())), preferred_element_type=jnp.float32
    )
    grad_h = lax.dot_general(
        grad_a, w_in, (((1,), (1,)), ((), ())), preferred_element_type=jnp.float32
    )
    ln_acc[...] += jnp.sum(grad_h * normed, axis=0, keepdims=True)
    scaled = grad_h * gain_ref[...]
    inner_mean = jnp.mean(scaled * normed, axis=1, keepdims=True)
    grad_x = inverse * (scaled - jnp.mean(scaled, axis=1, keepdims=True) - normed * inner_mean)
    grad_frames_ref[...] = keep_live(grad_x, masks, span).astype(jnp.bfloat16)

    @pl.when(step == pl.num_programs(0) - 1)
    def _():
        owners = packed_ref.shape[0]
        share = width // owners
        wide = w_in.shape[1] // LANES
        for c in range(blocks):
            flat[...] = jnp.zeros_like(flat)
            for k in range(taps):
                flat[k : k + 1] = jnp.sum(w_acc[c, k], axis=0, keepdims=True)
            flat[taps : taps + 1] = ln_acc[:, lane(c)]
            turned = flat[...].T.astype(jnp.bfloat16)
            for i in range(LANES // share):
                packed_ref[c * (LANES // share) + i, (wide + blocks) * share :] = turned[
                    i * share : (i + 1) * share
                ]
        for j in range(owners):
            rows = slice(j * share, (j + 1) * share)
            for c in range(wide):
                packed_ref[j, c * share : (c + 1) * share] = win_acc[rows, lane(c)].astype(
                    jnp.bfloat16
                )
            for c in range(blocks):
                packed_ref[j, (wide + c) * share : (wide + c + 1) * share] = wout_ref[
                    rows, lane(c)
                ].astype(jnp.bfloat16)


def plan_kernel(slots, lens_ref, owners_ref, up_ref, out_ref, meta_ref, stage, counts):
    me = lax.axis_index("bucket")
    own_rows, width = up_ref.shape
    span = out_ref.shape[1]
    blocks = width // LANES
    loaders = lens_ref.shape[1] // slots
    pairs = slots // loaders
    for c in range(blocks):
        stage[c, :own_rows] = up_ref[:, lane(c)].astype(jnp.float32)
        stage[c, own_rows:] = jnp.zeros((span, LANES), jnp.float32)

    def look(i, carry):
        found, start = carry
        mine = owners_ref[0, i] == me

        @pl.when(mine)
        def _():
            meta_ref[2, found] = start
            for c in range(blocks):
                out_ref[found, :, lane(c)] = stage[c, pl.ds(start, span)].astype(jnp.bfloat16)

        return found + mine.astype(jnp.int32), start + jnp.where(mine, lens_ref[0, i], 0)

    lax.fori_loop(0, loaders * slots, look, (jnp.int32(0), jnp.int32(0)))

    def clear(i, carry):
        counts[i] = 0
        return carry

    lax.fori_loop(0, loaders, clear, 0)

    def place(i, carry):
        owner = owners_ref[0, me * slots + i]
        rank = counts[owner]
        counts[owner] = rank + 1
        meta_ref[0, i] = lens_ref[0, me * slots + i]
        meta_ref[1, i] = owner * pairs + rank
        return carry

    lax.fori_loop(0, slots, place, 0)


def finish_kernel(meta_ref, arrived_ref, reduced_ref, out_ref, win_ref, wout_ref, last_ref, stage):
    slots, span, width = arrived_ref.shape
    own_rows = out_ref.shape[0]
    blocks = width // LANES
    wide = win_ref.shape[1] // LANES

    def place(u, carry):
        start = meta_ref[2, u]
        for c in range(blocks):
            stage[c, pl.ds(start, span)] = arrived_ref[u, :, lane(c)].astype(jnp.float32)
        return carry

    lax.fori_loop(0, slots, place, 0)
    for c in range(blocks):
        out_ref[:, lane(c)] = stage[c, :own_rows].astype(jnp.bfloat16)
        wout_ref[:, lane(c)] = reduced_ref[wide + c].astype(jnp.float32)
    for c in range(wide):
        win_ref[:, lane(c)] = reduced_ref[c].astype(jnp.float32)
    last_ref[...] = reduced_ref[wide + blocks].astype(jnp.float32)


def whole(shape):
    return pl.BlockSpec(shape, lambda i, *_: (0,) * len(shape))


def sum_kernel(groups, owners, part_ref, out_ref, slots, send_sems, recv_sems):
    count = groups * owners
    me = lax.axis_index("dp") * owners + lax.axis_index("bucket")
    barrier = pltpu.get_barrier_semaphore()

    def peer_of(i):
        other = lax.rem(me + i, count)
        return (other // owners, lax.rem(other, owners))

    def greet(i, carry):
        pl.semaphore_signal(barrier, inc=1, device_id=peer_of(i), device_id_type=MESH)
        return carry

    lax.fori_loop(1, count, greet, 0)
    pl.semaphore_wait(barrier, count - 1)

    def copy_to(i):
        return pltpu.make_async_remote_copy(
            src_ref=part_ref,
            dst_ref=slots.at[me],
            send_sem=send_sems.at[i],
            recv_sem=recv_sems.at[me],
            device_id=peer_of(i),
            device_id_type=MESH,
        )

    def send(i, carry):
        copy_to(i).start()
        return carry

    lax.fori_loop(1, count, send, 0)
    slots[me] = part_ref[...]

    def receive(i, carry):
        source = lax.rem(me + i, count)
        pltpu.make_async_remote_copy(
            src_ref=part_ref,
            dst_ref=slots.at[source],
            send_sem=send_sems.at[i],
            recv_sem=recv_sems.at[source],
            device_id=peer_of(i),
            device_id_type=MESH,
        ).wait_recv()
        return carry

    lax.fori_loop(1, count, receive, 0)
    out_ref[...] = lax.fori_loop(
        1, count, lambda i, total: total + slots[i], slots[0]
    )

    def sent(i, carry):
        copy_to(i).wait_send()
        return carry

    lax.fori_loop(1, count, sent, 0)


def sum_everywhere(part, collective_id):
    groups, owners = lax.axis_size("dp"), lax.axis_size("bucket")
    count = groups * owners
    return pl.pallas_call(
        functools.partial(sum_kernel, groups, owners),
        out_shape=jax.ShapeDtypeStruct(part.shape, part.dtype),
        in_specs=[pl.BlockSpec(memory_space=pltpu.VMEM)],
        out_specs=pl.BlockSpec(memory_space=pltpu.VMEM),
        scratch_shapes=[
            pltpu.VMEM((count,) + part.shape, part.dtype),
            pltpu.SemaphoreType.DMA((count,)),
            pltpu.SemaphoreType.DMA((count,)),
        ],
        compiler_params=pltpu.CompilerParams(collective_id=collective_id, has_side_effects=True),
        cost_estimate=pl.CostEstimate(flops=10**6, bytes_accessed=2 * 10**7, transcendentals=0),
        name="sum_everywhere_%d" % collective_id,
    )(part)


def reduce_kernel(groups, owners, src, out, first, first_sum, second, second_sum, third, mine,
                  core_sems, pair_sems, row_sems, all_sems):
    dp, me = lax.axis_index("dp"), lax.axis_index("bucket")
    halves = groups // 2
    core, side = lax.rem(dp, 2), dp // 2
    chunk = core * halves + side
    partner = side * 2 + (1 - core)
    barrier = pltpu.get_barrier_semaphore()

    def group_peer(i):
        return lax.rem(dp + i, groups)

    def owner_peer(i):
        return lax.rem(me + i, owners)

    def greet_group(i, carry):
        pl.semaphore_signal(barrier, inc=1, device_id=(group_peer(i), me), device_id_type=MESH)
        return carry

    def greet_owner(i, carry):
        pl.semaphore_signal(barrier, inc=1, device_id=(dp, owner_peer(i)), device_id_type=MESH)
        return carry

    lax.fori_loop(1, groups, greet_group, 0)
    lax.fori_loop(1, owners, greet_owner, 0)
    pl.semaphore_wait(barrier, groups + owners - 2)

    def remote(source, target, sems, i, j, device):
        return pltpu.make_async_remote_copy(
            src_ref=source,
            dst_ref=target,
            send_sem=sems.at[0, i],
            recv_sem=sems.at[1, j],
            device_id=device,
            device_id_type=MESH,
        )

    def bucket_of(i):
        return lax.rem(me + 1 + i, owners)

    def swap(i):
        bucket = bucket_of(i)
        return remote(src.at[bucket, 1 - core], first.at[bucket], core_sems, i, i, (partner, me))

    def to_side(i, n, arriving):
        bucket = bucket_of(i)
        other = lax.rem(side + n, halves)
        slot = other if arriving else side
        return remote(
            first_sum.at[bucket, other], second.at[slot, bucket], pair_sems,
            n * owners + i, slot * owners + i, (other * 2 + core, me),
        )

    def to_owner(i, arriving):
        other = owner_peer(i)
        slot = other if arriving else me
        return remote(second_sum.at[other], third.at[slot], row_sems, i, slot, (dp, other))

    def start_swap(i, carry):
        swap(i).start()
        return carry

    def add_first(i, carry):
        bucket = bucket_of(i)
        swap(i).wait_recv()
        total = src[bucket, core].astype(jnp.float32) + first[bucket].astype(jnp.float32)
        first_sum[bucket] = total.astype(jnp.bfloat16)
        for n in range(1, halves):
            to_side(i, n, False).start()
        return carry

    def add_second(i, carry):
        bucket = bucket_of(i)
        total = first_sum[bucket, side].astype(jnp.float32)
        for n in range(1, halves):
            to_side(i, n, True).wait_recv()
            total = total + second[lax.rem(side + n, halves), bucket].astype(jnp.float32)
        second_sum[bucket] = total.astype(jnp.bfloat16)
        return carry

    def add_and_send(i, carry):
        add_second(i, carry)
        to_owner(i + 1, False).start()
        return carry

    def wait_owner(i, carry):
        to_owner(i, True).wait_recv()
        return carry

    lax.fori_loop(0, owners, start_swap, 0)
    lax.fori_loop(0, owners, add_first, 0)
    lax.fori_loop(0, owners - 1, add_and_send, 0)
    add_second(owners - 1, 0)
    third[me] = second_sum[me]
    lax.fori_loop(1, owners, wait_owner, 0)
    total = lax.fori_loop(
        1, owners, lambda i, t: t + third[i].astype(jnp.float32), third[0].astype(jnp.float32)
    )
    mine[...] = total.astype(jnp.bfloat16)

    def to_group(i, arriving):
        other = group_peer(i)
        device = other if arriving else dp
        slot = lax.rem(device, 2) * halves + device // 2
        return remote(mine, out.at[slot], all_sems, i, slot, (other, me))

    def send_group(i, carry):
        to_group(i, False).start()
        return carry

    def wait_group(i, carry):
        to_group(i, True).wait_recv()
        return carry

    lax.fori_loop(1, groups, send_group, 0)
    out[chunk] = mine[...]
    lax.fori_loop(1, groups, wait_group, 0)

    def sent_owner(i, carry):
        to_owner(i, False).wait_send()
        return carry

    def sent_group(i, carry):
        to_group(i, False).wait_send()
        return carry

    def sent_first(i, carry):
        swap(i).wait_send()
        for n in range(1, halves):
            to_side(i, n, False).wait_send()
        return carry

    lax.fori_loop(0, owners, sent_first, 0)
    lax.fori_loop(1, owners, sent_owner, 0)
    lax.fori_loop(1, groups, sent_group, 0)


def reduce_rows(packed, collective_id):
    groups, owners = lax.axis_size("dp"), lax.axis_size("bucket")
    halves = groups // 2
    rows = packed.shape[1] // groups
    source = packed.reshape(owners, 2, halves, rows, LANES)
    kind = jnp.bfloat16
    return pl.pallas_call(
        functools.partial(reduce_kernel, groups, owners),
        out_shape=jax.ShapeDtypeStruct((groups, rows, LANES), kind),
        in_specs=[pl.BlockSpec(memory_space=pltpu.VMEM)],
        out_specs=pl.BlockSpec(memory_space=pltpu.VMEM),
        scratch_shapes=[
            pltpu.VMEM((owners, halves, rows, LANES), kind),
            pltpu.VMEM((owners, halves, rows, LANES), kind),
            pltpu.VMEM((halves, owners, rows, LANES), kind),
            pltpu.VMEM((owners, rows, LANES), kind),
            pltpu.VMEM((owners, rows, LANES), kind),
            pltpu.VMEM((rows, LANES), kind),
            pltpu.SemaphoreType.DMA((2, owners)),
            pltpu.SemaphoreType.DMA((2, halves * owners)),
            pltpu.SemaphoreType.DMA((2, owners)),
            pltpu.SemaphoreType.DMA((2, groups)),
        ],
        compiler_params=pltpu.CompilerParams(collective_id=collective_id, has_side_effects=True),
        cost_estimate=pl.CostEstimate(flops=10**7, bytes_accessed=6 * 10**7, transcendentals=0),
        name="reduce_rows",
    )(source)


def local(frames, lengths, owners, upstream, ln_gain, w_in, w_dw, bn_gain, bn_bias, w_out):
    loaders = lax.axis_size("bucket")
    width = frames.shape[1]
    taps = w_dw.shape[1]
    slot_count = lengths.shape[1] // loaders
    span = frames.shape[0] // slot_count
    pair_count = slot_count // loaders
    own_rows = upstream.shape[0]
    blocks = width // LANES
    total_frames = float(own_rows * loaders * lax.axis_size("dp"))
    stage_shape = pltpu.VMEM((blocks, own_rows + span, LANES), jnp.float32)
    slot_shape = jax.ShapeDtypeStruct((slot_count, span, width), jnp.bfloat16)
    in_vmem = pl.BlockSpec(memory_space=pltpu.VMEM)
    in_smem = pl.BlockSpec(memory_space=pltpu.SMEM)
    outgoing, meta = pl.pallas_call(
        functools.partial(plan_kernel, slot_count),
        in_specs=[in_smem, in_smem, in_vmem],
        out_specs=[in_vmem, in_smem],
        out_shape=[slot_shape, jax.ShapeDtypeStruct((3, slot_count), jnp.int32)],
        scratch_shapes=[stage_shape, pltpu.SMEM((loaders,), jnp.int32)],
        compiler_params=pltpu.CompilerParams(vmem_limit_bytes=VMEM_LIMIT),
        name="plan",
    )(lengths, owners, upstream)

    def exchange(slots):
        slots = slots.reshape(loaders, pair_count, span, width)
        moved = lax.all_to_all(slots, "bucket", split_axis=0, concat_axis=0, tiled=True)
        return moved.reshape(slot_count, span, width)

    incoming = exchange(outgoing)

    group = 4
    steps = slot_count // group
    rows = group * span
    edge = (taps + 1) // 2
    row_block = pl.BlockSpec((rows, width), lambda i, *_: (i, 0))
    all_rows = slot_count * span
    gain_row, bn_gain_row, bn_bias_row = ln_gain[None], bn_gain[None], bn_bias[None]
    w_taps = jnp.pad(w_dw.T, ((0, 1), (0, 0)))
    sums_shape = (2 * blocks, LANES)
    params = pltpu.CompilerParams(
        dimension_semantics=("arbitrary",), vmem_limit_bytes=VMEM_LIMIT
    )
    padded_shape = pltpu.VMEM((group, blocks, span + 2 * edge, LANES), jnp.float32)

    conv, part = pl.pallas_call(
        functools.partial(forward_kernel, group, span, taps),
        grid_spec=pltpu.PrefetchScalarGridSpec(
            num_scalar_prefetch=1,
            grid=(steps,),
            in_specs=[row_block, whole((1, width)), whole(w_in.shape), whole(w_taps.shape)],
            out_specs=[row_block, whole(sums_shape)],
            scratch_shapes=[padded_shape],
        ),
        out_shape=[
            jax.ShapeDtypeStruct((all_rows, width), jnp.float32),
            jax.ShapeDtypeStruct(sums_shape, jnp.float32),
        ],
        compiler_params=params,
        cost_estimate=pl.CostEstimate(
            flops=2 * 10**9, bytes_accessed=4 * 10**7, transcendentals=0
        ),
        name="forward",
    )(meta, frames, gain_row, w_in, w_taps)
    totals = sum_everywhere(part, 0)

    out_rows, grad_bn, back_part, grad_wout = pl.pallas_call(
        functools.partial(middle_kernel, group, span, total_frames),
        grid_spec=pltpu.PrefetchScalarGridSpec(
            num_scalar_prefetch=1,
            grid=(steps,),
            in_specs=[
                row_block, whole(slot_shape.shape), whole(sums_shape), whole((1, width)),
                whole((1, width)), whole(w_out.shape),
            ],
            out_specs=[whole(slot_shape.shape), row_block, whole(sums_shape), whole(w_out.shape)],
        ),
        out_shape=[
            slot_shape,
            jax.ShapeDtypeStruct((all_rows, width), jnp.float32),
            jax.ShapeDtypeStruct(sums_shape, jnp.float32),
            jax.ShapeDtypeStruct(w_out.shape, jnp.float32),
        ],
        compiler_params=params,
        cost_estimate=pl.CostEstimate(
            flops=3 * 10**9, bytes_accessed=2 * 10**7, transcendentals=0
        ),
        name="middle",
    )(meta, conv, incoming, totals, bn_gain_row, bn_bias_row, w_out)

    back_totals = sum_everywhere(back_part, 1)
    leaving, back_totals = lax.optimization_barrier((out_rows, back_totals))
    arrived = exchange(leaving)

    share = width // loaders
    packed_rows = (w_in.shape[1] // LANES + blocks + 1) * share
    grad_frames, packed = pl.pallas_call(
        functools.partial(backward_kernel, group, span, taps, total_frames),
        grid_spec=pltpu.PrefetchScalarGridSpec(
            num_scalar_prefetch=1,
            grid=(steps,),
            in_specs=[
                row_block, row_block, row_block, whole(sums_shape), whole(sums_shape),
                whole((1, width)), whole((1, width)), whole(w_in.shape), whole(w_taps.shape),
                whole(w_out.shape),
            ],
            out_specs=[row_block, whole((loaders, packed_rows, LANES))],
            scratch_shapes=[
                padded_shape,
                padded_shape,
                pltpu.VMEM((rows, width), jnp.float32),
                pltpu.VMEM((blocks, taps + 1, SUB, LANES), jnp.float32),
                pltpu.VMEM(w_in.shape, jnp.float32),
                pltpu.VMEM((1, width), jnp.float32),
                pltpu.VMEM((LANES, LANES), jnp.float32),
            ],
        ),
        out_shape=[
            jax.ShapeDtypeStruct((all_rows, width), jnp.bfloat16),
            jax.ShapeDtypeStruct((loaders, packed_rows, LANES), jnp.bfloat16),
        ],
        compiler_params=params,
        cost_estimate=pl.CostEstimate(
            flops=6 * 10**9, bytes_accessed=8 * 10**7, transcendentals=0
        ),
        name="backward",
    )(
        meta, frames, conv, grad_bn, totals, back_totals, gain_row, bn_gain_row, w_in, w_taps,
        grad_wout,
    )
    reduced = reduce_rows(packed, 2).reshape(-1, share, LANES)
    out_frames, grad_win, grad_wo, last = pl.pallas_call(
        finish_kernel,
        in_specs=[in_smem, in_vmem, in_vmem],
        out_specs=[in_vmem] * 4,
        out_shape=[
            jax.ShapeDtypeStruct((own_rows, width), jnp.bfloat16),
            jax.ShapeDtypeStruct((share, w_in.shape[1]), jnp.float32),
            jax.ShapeDtypeStruct((share, width), jnp.float32),
            jax.ShapeDtypeStruct((share, LANES), jnp.float32),
        ],
        scratch_shapes=[stage_shape],
        compiler_params=pltpu.CompilerParams(vmem_limit_bytes=VMEM_LIMIT),
        name="finish",
    )(meta, arrived, reduced)
    flat_back = back_totals.reshape(2, width)
    return (
        out_frames,
        grad_frames,
        grad_win,
        grad_wo,
        last[:, :taps],
        last[:, taps],
        flat_back[1],
        flat_back[0],
    )


def solution(mesh):
    placed = (
        P(("dp", "bucket"), None),
        P("dp", None),
        P("dp", None),
        P(("dp", "bucket"), None),
        P(),
        P(),
        P(),
        P(),
        P(),
        P(),
    )
    return jax.shard_map(
        local,
        mesh=mesh,
        in_specs=placed,
        out_specs=(
            P(("dp", "bucket"), None),
            P(("dp", "bucket"), None),
            P("bucket", None),
            P("bucket", None),
            P("bucket", None),
            P("bucket"),
            P(),
            P(),
        ),
        check_vma=False,
    )
```

```python
import functools

import jax
import jax.numpy as jnp
from jax import lax
from jax.experimental import pallas as pl
from jax.experimental.pallas import tpu as pltpu
from jax.sharding import PartitionSpec as P

EPSILON = 1e-05
LANES = 128
SUB = 8
MESH = pl.DeviceIdType.MESH
VMEM_LIMIT = 24 << 20


def lane(c):
    return slice(c * LANES, (c + 1) * LANES)


def row_of(packed, first, blocks):
    return jnp.concatenate([packed[first + c : first + c + 1] for c in range(blocks)], axis=1)


def live_rows(lens_ref, first, count, span, width):
    position = lax.broadcasted_iota(jnp.int32, (span, width), 0)
    return [position < lens_ref[0, first + i] for i in range(count)]


def keep_live(values, masks, span):
    parts = [
        jnp.where(masks[i], values[i * span : (i + 1) * span], 0.0) for i in range(len(masks))
    ]
    return jnp.concatenate(parts, axis=0)


def layer_norm(frame_rows):
    values = frame_rows.astype(jnp.float32)
    centred = values - jnp.mean(values, axis=1, keepdims=True)
    inverse = lax.rsqrt(jnp.mean(centred * centred, axis=1, keepdims=True) + EPSILON)
    return centred * inverse, inverse


def project(frame_rows, gain, w_in):
    normed, inverse = layer_norm(frame_rows)
    h = (normed * gain).astype(jnp.bfloat16)
    projected = jnp.dot(h, w_in, preferred_element_type=jnp.float32)
    half = projected.shape[1] // 2
    return normed, inverse, projected[:, :half], jax.nn.sigmoid(projected[:, half:])


def shifted_sum(frame, weight, span, taps):
    lead = (taps + 1) // 2 // SUB
    count = span // SUB
    tiles = [frame[i * SUB : (i + 1) * SUB] for i in range(count)]
    total = None
    for residue in range(SUB):
        shifts = [k for k in range(residue, taps + 1, SUB) if k > 0]
        weights = {k: jnp.broadcast_to(weight(k), (SUB, LANES)) for k in shifts}
        parts = []
        for i in range(count + 1 if residue else count):
            part = None
            for k in shifts:
                at = (k - residue) // SUB + i - lead
                if 0 <= at < count:
                    term = tiles[at] * weights[k]
                    part = term if part is None else part + term
            parts.append(jnp.zeros((SUB, LANES), jnp.float32) if part is None else part)
        moved = jnp.concatenate(parts, axis=0)
        if residue:
            moved = pltpu.roll(moved, span + SUB - residue, 0)[:span]
        total = moved if total is None else total + moved
    return total


def forward_kernel(group, span, taps, lens_ref, frames_ref, gain_ref, w_in_ref, w_dw_ref,
                   conv_ref, sums_ref, normed_ref, inverse_ref, linear_ref, gate_ref, padded):
    step = pl.program_id(0)
    blocks = conv_ref.shape[1] // LANES

    @pl.when(step == 0)
    def _():
        sums_ref[...] = jnp.zeros_like(sums_ref)

    masks = live_rows(lens_ref, step * group, group, span, conv_ref.shape[1])
    normed, inverse, linear, gate = project(frames_ref[...], gain_ref[...], w_in_ref[...])
    normed_ref[...] = normed
    inverse_ref[...] = jnp.broadcast_to(inverse, inverse_ref.shape)
    linear_ref[...] = linear
    gate_ref[...] = gate
    gated = keep_live(linear * gate, masks, span).astype(jnp.bfloat16).astype(jnp.float32)
    for u in range(group):
        for c in range(blocks):
            padded[u, c] = gated[u * span : (u + 1) * span, lane(c)]

    def one(u, carry):
        live = lax.broadcasted_iota(jnp.int32, (span, LANES), 0) < lens_ref[0, step * group + u]
        start = pl.multiple_of(u * span, SUB)
        for c in range(blocks):
            conv = shifted_sum(
                padded[u, c], lambda k: w_dw_ref[k - 1 : k, lane(c)], span, taps
            )
            conv_ref[pl.ds(start, span), lane(c)] = conv
            masked = jnp.where(live, conv, 0.0)
            sums_ref[c : c + 1] += jnp.sum(masked, axis=0, keepdims=True)
            sums_ref[blocks + c : blocks + c + 1] += jnp.sum(
                masked * masked, axis=0, keepdims=True
            )
        return carry

    lax.fori_loop(0, group, one, 0)


def batch_norm(total_ref, conv, total_frames, blocks):
    packed = total_ref[...]
    centre = row_of(packed, 0, blocks) / total_frames
    variance = row_of(packed, blocks, blocks) / total_frames - centre * centre
    inverse = lax.rsqrt(variance + EPSILON)
    return (conv - centre) * inverse, inverse


def middle_kernel(group, span, total_frames, lens_ref, conv_ref, dy_ref, total_ref, bn_gain_ref,
                  bn_bias_ref, w_out_ref, out_ref, grad_bn_ref, sums_ref, grad_wout_ref):
    step = pl.program_id(0)
    width = conv_ref.shape[1]
    blocks = width // LANES

    @pl.when(step == 0)
    def _():
        sums_ref[...] = jnp.zeros_like(sums_ref)
        grad_wout_ref[...] = jnp.zeros_like(grad_wout_ref)

    masks = live_rows(lens_ref, step * group, group, span, width)
    slots = [lens_ref[1, step * group + i] for i in range(group)]
    arrived = jnp.concatenate([dy_ref[slot] for slot in slots], axis=0)
    dy = keep_live(arrived.astype(jnp.float32), masks, span).astype(jnp.bfloat16)
    w_out = w_out_ref[...]
    bn_normed, _ = batch_norm(total_ref, conv_ref[...], total_frames, blocks)
    bn = bn_normed * bn_gain_ref[...] + bn_bias_ref[...]
    sig = jax.nn.sigmoid(bn)
    swished = (bn * sig).astype(jnp.bfloat16)
    out = jnp.dot(swished, w_out, preferred_element_type=jnp.float32).astype(jnp.bfloat16)
    for i in range(group):
        out_ref[slots[i]] = out[i * span : (i + 1) * span]
    grad_wout_ref[...] += lax.dot_general(
        swished, dy, (((0,), (0,)), ((), ())), preferred_element_type=jnp.float32
    )
    grad_swish = lax.dot_general(
        dy, w_out, (((1,), (1,)), ((), ())), preferred_element_type=jnp.float32
    )
    grad_bn = grad_swish * (sig * (1.0 + bn * (1.0 - sig)))
    grad_bn_ref[...] = grad_bn
    bias_row = jnp.sum(grad_bn, axis=0, keepdims=True)
    gain_row = jnp.sum(grad_bn * bn_normed, axis=0, keepdims=True)
    for c in range(blocks):
        sums_ref[c : c + 1] += bias_row[:, lane(c)]
        sums_ref[blocks + c : blocks + c + 1] += gain_row[:, lane(c)]


def backward_kernel(group, span, taps, total_frames, lens_ref, normed_ref, inverse_ref,
                    linear_ref, gate_ref, conv_ref, grad_bn_ref,
                    total_ref, back_ref, gain_ref, bn_gain_ref, w_in_ref, w_dw_ref, wout_ref,
                    grad_frames_ref, packed_ref, padded, grad_pad, gated_grad, w_acc, win_acc,
                    ln_acc, flat):
    step = pl.program_id(0)
    width = conv_ref.shape[1]
    blocks = width // LANES
    count = span // SUB
    lead = (taps + 1) // 2 // SUB

    @pl.when(step == 0)
    def _():
        w_acc[...] = jnp.zeros_like(w_acc)
        win_acc[...] = jnp.zeros_like(win_acc)
        ln_acc[...] = jnp.zeros_like(ln_acc)

    masks = live_rows(lens_ref, step * group, group, span, width)
    w_in = w_in_ref[...]
    gated = keep_live(linear_ref[...] * gate_ref[...], masks, span).astype(jnp.bfloat16).astype(jnp.float32)
    bn_normed, bn_inverse = batch_norm(total_ref, conv_ref[...], total_frames, blocks)
    back = back_ref[...]
    bias_mean = row_of(back, 0, blocks) / total_frames
    gain_mean = row_of(back, blocks, blocks) / total_frames
    grad_conv = keep_live(
        bn_gain_ref[...] * bn_inverse * (grad_bn_ref[...] - bias_mean - bn_normed * gain_mean),
        masks,
        span,
    )
    for u in range(group):
        for c in range(blocks):
            rows = slice(u * span, (u + 1) * span)
            padded[u, c] = gated[rows, lane(c)]
            grad_pad[u, c] = grad_conv[rows, lane(c)]

    def one(u, carry):
        start = pl.multiple_of(u * span, SUB)
        for c in range(blocks):
            grads = grad_pad[u, c]
            gated_grad[pl.ds(start, span), lane(c)] = shifted_sum(
                grads, lambda k: w_dw_ref[taps - k : taps - k + 1, lane(c)], span, taps
            )
            blank = jnp.zeros((SUB, LANES), jnp.float32)
            inner = jnp.concatenate([blank, grads, blank], axis=0)
            frame = padded[u, c]
            for residue in range(SUB):
                moved = inner if residue == 0 else pltpu.roll(inner, residue, 0)
                moved = moved[SUB:]
                for k in range(residue, taps + 1, SUB):
                    if k == 0:
                        continue
                    part = None
                    for i in range(count + 1 if residue else count):
                        at = (k - residue) // SUB + i - lead
                        if 0 <= at < count:
                            tile = frame[at * SUB : (at + 1) * SUB]
                            term = moved[i * SUB : (i + 1) * SUB] * tile
                            part = term if part is None else part + term
                    w_acc[c, k - 1] += part
        return carry

    lax.fori_loop(0, group, one, 0)

    grad_gated = keep_live(gated_grad[...], masks, span)
    linear, gate = linear_ref[...], gate_ref[...]
    normed, inverse = normed_ref[...], inverse_ref[:, :1]
    h = (normed * gain_ref[...]).astype(jnp.bfloat16)
    left = grad_gated * gate
    grad_a = jnp.concatenate(
        [left.astype(jnp.bfloat16), (left * linear * (1.0 - gate)).astype(jnp.bfloat16)], axis=1
    )
    win_acc[...] += lax.dot_general(
        h, grad_a, (((0,), (0,)), ((), ())), preferred_element_type=jnp.float32
    )
    grad_h = lax.dot_general(
        grad_a, w_in, (((1,), (1,)), ((), ())), preferred_element_type=jnp.float32
    )
    ln_acc[...] += jnp.sum(grad_h * normed, axis=0, keepdims=True)
    scaled = grad_h * gain_ref[...]
    inner_mean = jnp.mean(scaled * normed, axis=1, keepdims=True)
    grad_x = inverse * (scaled - jnp.mean(scaled, axis=1, keepdims=True) - normed * inner_mean)
    grad_frames_ref[...] = keep_live(grad_x, masks, span).astype(jnp.bfloat16)

    @pl.when(step == pl.num_programs(0) - 1)
    def _():
        owners = packed_ref.shape[0]
        share = width // owners
        wide = w_in.shape[1] // LANES
        for c in range(blocks):
            flat[...] = jnp.zeros_like(flat)
            for k in range(taps):
                flat[k : k + 1] = jnp.sum(w_acc[c, k], axis=0, keepdims=True)
            flat[taps : taps + 1] = ln_acc[:, lane(c)]
            turned = flat[...].T.astype(jnp.bfloat16)
            for i in range(LANES // share):
                packed_ref[c * (LANES // share) + i, (wide + blocks) * share :] = turned[
                    i * share : (i + 1) * share
                ]
        for j in range(owners):
            rows = slice(j * share, (j + 1) * share)
            for c in range(wide):
                packed_ref[j, c * share : (c + 1) * share] = win_acc[rows, lane(c)].astype(
                    jnp.bfloat16
                )
            for c in range(blocks):
                packed_ref[j, (wide + c) * share : (wide + c + 1) * share] = wout_ref[
                    rows, lane(c)
                ].astype(jnp.bfloat16)


def plan_kernel(slots, lens_ref, owners_ref, up_ref, out_ref, meta_ref, stage, counts):
    me = lax.axis_index("bucket")
    own_rows, width = up_ref.shape
    span = out_ref.shape[1]
    blocks = width // LANES
    loaders = lens_ref.shape[1] // slots
    pairs = slots // loaders
    for c in range(blocks):
        stage[c, :own_rows] = up_ref[:, lane(c)].astype(jnp.float32)
        stage[c, own_rows:] = jnp.zeros((span, LANES), jnp.float32)

    def look(i, carry):
        found, start = carry
        mine = owners_ref[0, i] == me

        @pl.when(mine)
        def _():
            meta_ref[2, found] = start
            for c in range(blocks):
                out_ref[found, :, lane(c)] = stage[c, pl.ds(start, span)].astype(jnp.bfloat16)

        return found + mine.astype(jnp.int32), start + jnp.where(mine, lens_ref[0, i], 0)

    lax.fori_loop(0, loaders * slots, look, (jnp.int32(0), jnp.int32(0)))

    def clear(i, carry):
        counts[i] = 0
        return carry

    lax.fori_loop(0, loaders, clear, 0)

    def place(i, carry):
        owner = owners_ref[0, me * slots + i]
        rank = counts[owner]
        counts[owner] = rank + 1
        meta_ref[0, i] = lens_ref[0, me * slots + i]
        meta_ref[1, i] = owner * pairs + rank
        return carry

    lax.fori_loop(0, slots, place, 0)


def finish_kernel(meta_ref, arrived_ref, reduced_ref, out_ref, win_ref, wout_ref, last_ref, stage):
    slots, span, width = arrived_ref.shape
    own_rows = out_ref.shape[0]
    blocks = width // LANES
    wide = win_ref.shape[1] // LANES

    def place(u, carry):
        start = meta_ref[2, u]
        for c in range(blocks):
            stage[c, pl.ds(start, span)] = arrived_ref[u, :, lane(c)].astype(jnp.float32)
        return carry

    lax.fori_loop(0, slots, place, 0)
    for c in range(blocks):
        out_ref[:, lane(c)] = stage[c, :own_rows].astype(jnp.bfloat16)
        wout_ref[:, lane(c)] = reduced_ref[wide + c].astype(jnp.float32)
    for c in range(wide):
        win_ref[:, lane(c)] = reduced_ref[c].astype(jnp.float32)
    last_ref[...] = reduced_ref[wide + blocks].astype(jnp.float32)


def whole(shape):
    return pl.BlockSpec(shape, lambda i, *_: (0,) * len(shape))


def sum_kernel(groups, owners, part_ref, out_ref, slots, send_sems, recv_sems):
    count = groups * owners
    me = lax.axis_index("dp") * owners + lax.axis_index("bucket")
    barrier = pltpu.get_barrier_semaphore()

    def peer_of(i):
        other = lax.rem(me + i, count)
        return (other // owners, lax.rem(other, owners))

    def greet(i, carry):
        pl.semaphore_signal(barrier, inc=1, device_id=peer_of(i), device_id_type=MESH)
        return carry

    lax.fori_loop(1, count, greet, 0)
    pl.semaphore_wait(barrier, count - 1)

    def copy_to(i):
        return pltpu.make_async_remote_copy(
            src_ref=part_ref,
            dst_ref=slots.at[me],
            send_sem=send_sems.at[i],
            recv_sem=recv_sems.at[me],
            device_id=peer_of(i),
            device_id_type=MESH,
        )

    def send(i, carry):
        copy_to(i).start()
        return carry

    lax.fori_loop(1, count, send, 0)
    slots[me] = part_ref[...]

    def receive(i, carry):
        source = lax.rem(me + i, count)
        pltpu.make_async_remote_copy(
            src_ref=part_ref,
            dst_ref=slots.at[source],
            send_sem=send_sems.at[i],
            recv_sem=recv_sems.at[source],
            device_id=peer_of(i),
            device_id_type=MESH,
        ).wait_recv()
        return carry

    lax.fori_loop(1, count, receive, 0)
    out_ref[...] = lax.fori_loop(
        1, count, lambda i, total: total + slots[i], slots[0]
    )

    def sent(i, carry):
        copy_to(i).wait_send()
        return carry

    lax.fori_loop(1, count, sent, 0)


def sum_everywhere(part, collective_id):
    groups, owners = lax.axis_size("dp"), lax.axis_size("bucket")
    count = groups * owners
    return pl.pallas_call(
        functools.partial(sum_kernel, groups, owners),
        out_shape=jax.ShapeDtypeStruct(part.shape, part.dtype),
        in_specs=[pl.BlockSpec(memory_space=pltpu.VMEM)],
        out_specs=pl.BlockSpec(memory_space=pltpu.VMEM),
        scratch_shapes=[
            pltpu.VMEM((count,) + part.shape, part.dtype),
            pltpu.SemaphoreType.DMA((count,)),
            pltpu.SemaphoreType.DMA((count,)),
        ],
        compiler_params=pltpu.CompilerParams(
            collective_id=collective_id, has_side_effects=True, vmem_limit_bytes=4 << 20
        ),
        cost_estimate=pl.CostEstimate(flops=10**6, bytes_accessed=2 * 10**7, transcendentals=0),
        name="sum_everywhere_%d" % collective_id,
    )(part)


def reduce_kernel(groups, owners, src, out, first, first_sum, second, second_sum, third, mine,
                  core_sems, pair_sems, row_sems, all_sems):
    dp, me = lax.axis_index("dp"), lax.axis_index("bucket")
    halves = groups // 2
    core, side = lax.rem(dp, 2), dp // 2
    chunk = core * halves + side
    partner = side * 2 + (1 - core)
    barrier = pltpu.get_barrier_semaphore()

    def group_peer(i):
        return lax.rem(dp + i, groups)

    def owner_peer(i):
        return lax.rem(me + i, owners)

    def greet_group(i, carry):
        pl.semaphore_signal(barrier, inc=1, device_id=(group_peer(i), me), device_id_type=MESH)
        return carry

    def greet_owner(i, carry):
        pl.semaphore_signal(barrier, inc=1, device_id=(dp, owner_peer(i)), device_id_type=MESH)
        return carry

    lax.fori_loop(1, groups, greet_group, 0)
    lax.fori_loop(1, owners, greet_owner, 0)
    pl.semaphore_wait(barrier, groups + owners - 2)

    def remote(source, target, sems, i, j, device):
        return pltpu.make_async_remote_copy(
            src_ref=source,
            dst_ref=target,
            send_sem=sems.at[0, i],
            recv_sem=sems.at[1, j],
            device_id=device,
            device_id_type=MESH,
        )

    def bucket_of(i):
        return lax.rem(me + 1 + i, owners)

    def swap(i):
        bucket = bucket_of(i)
        return remote(src.at[bucket, 1 - core], first.at[bucket], core_sems, i, i, (partner, me))

    def to_side(i, n, arriving):
        bucket = bucket_of(i)
        other = lax.rem(side + n, halves)
        slot = other if arriving else side
        return remote(
            first_sum.at[bucket, other], second.at[slot, bucket], pair_sems,
            n * owners + i, slot * owners + i, (other * 2 + core, me),
        )

    def to_owner(i, arriving):
        other = owner_peer(i)
        slot = other if arriving else me
        return remote(second_sum.at[other], third.at[slot], row_sems, i, slot, (dp, other))

    def start_swap(i, carry):
        swap(i).start()
        return carry

    def add_first(i, carry):
        bucket = bucket_of(i)
        swap(i).wait_recv()
        total = src[bucket, core].astype(jnp.float32) + first[bucket].astype(jnp.float32)
        first_sum[bucket] = total.astype(jnp.bfloat16)
        for n in range(1, halves):
            to_side(i, n, False).start()
        return carry

    def add_second(i, carry):
        bucket = bucket_of(i)
        total = first_sum[bucket, side].astype(jnp.float32)
        for n in range(1, halves):
            to_side(i, n, True).wait_recv()
            total = total + second[lax.rem(side + n, halves), bucket].astype(jnp.float32)
        second_sum[bucket] = total.astype(jnp.bfloat16)
        return carry

    def add_and_send(i, carry):
        add_second(i, carry)
        to_owner(i + 1, False).start()
        return carry

    def wait_owner(i, carry):
        to_owner(i, True).wait_recv()
        return carry

    lax.fori_loop(0, owners, start_swap, 0)
    lax.fori_loop(0, owners, add_first, 0)
    lax.fori_loop(0, owners - 1, add_and_send, 0)
    add_second(owners - 1, 0)
    third[me] = second_sum[me]
    lax.fori_loop(1, owners, wait_owner, 0)
    total = lax.fori_loop(
        1, owners, lambda i, t: t + third[i].astype(jnp.float32), third[0].astype(jnp.float32)
    )
    mine[...] = total.astype(jnp.bfloat16)

    def to_group(i, arriving):
        other = group_peer(i)
        device = other if arriving else dp
        slot = lax.rem(device, 2) * halves + device // 2
        return remote(mine, out.at[slot], all_sems, i, slot, (other, me))

    def send_group(i, carry):
        to_group(i, False).start()
        return carry

    def wait_group(i, carry):
        to_group(i, True).wait_recv()
        return carry

    lax.fori_loop(1, groups, send_group, 0)
    out[chunk] = mine[...]
    lax.fori_loop(1, groups, wait_group, 0)

    def sent_owner(i, carry):
        to_owner(i, False).wait_send()
        return carry

    def sent_group(i, carry):
        to_group(i, False).wait_send()
        return carry

    def sent_first(i, carry):
        swap(i).wait_send()
        for n in range(1, halves):
            to_side(i, n, False).wait_send()
        return carry

    lax.fori_loop(0, owners, sent_first, 0)
    lax.fori_loop(1, owners, sent_owner, 0)
    lax.fori_loop(1, groups, sent_group, 0)


def reduce_rows(packed, collective_id):
    groups, owners = lax.axis_size("dp"), lax.axis_size("bucket")
    halves = groups // 2
    rows = packed.shape[1] // groups
    source = packed.reshape(owners, 2, halves, rows, LANES)
    kind = jnp.bfloat16
    return pl.pallas_call(
        functools.partial(reduce_kernel, groups, owners),
        out_shape=jax.ShapeDtypeStruct((groups, rows, LANES), kind),
        in_specs=[pl.BlockSpec(memory_space=pltpu.VMEM)],
        out_specs=pl.BlockSpec(memory_space=pltpu.VMEM),
        scratch_shapes=[
            pltpu.VMEM((owners, halves, rows, LANES), kind),
            pltpu.VMEM((owners, halves, rows, LANES), kind),
            pltpu.VMEM((halves, owners, rows, LANES), kind),
            pltpu.VMEM((owners, rows, LANES), kind),
            pltpu.VMEM((owners, rows, LANES), kind),
            pltpu.VMEM((rows, LANES), kind),
            pltpu.SemaphoreType.DMA((2, owners)),
            pltpu.SemaphoreType.DMA((2, halves * owners)),
            pltpu.SemaphoreType.DMA((2, owners)),
            pltpu.SemaphoreType.DMA((2, groups)),
        ],
        compiler_params=pltpu.CompilerParams(
            collective_id=collective_id, has_side_effects=True, vmem_limit_bytes=16 << 20
        ),
        cost_estimate=pl.CostEstimate(flops=10**7, bytes_accessed=6 * 10**7, transcendentals=0),
        name="reduce_rows",
    )(source)


def in_hbm(array):
    return pltpu.with_memory_space_constraint(array, pltpu.HBM)


def local(frames, lengths, owners, upstream, ln_gain, w_in, w_dw, bn_gain, bn_bias, w_out):
    loaders = lax.axis_size("bucket")
    width = frames.shape[1]
    taps = w_dw.shape[1]
    slot_count = lengths.shape[1] // loaders
    span = frames.shape[0] // slot_count
    pair_count = slot_count // loaders
    own_rows = upstream.shape[0]
    blocks = width // LANES
    total_frames = float(own_rows * loaders * lax.axis_size("dp"))
    stage_shape = pltpu.VMEM((blocks, own_rows + span, LANES), jnp.float32)
    slot_shape = jax.ShapeDtypeStruct((slot_count, span, width), jnp.bfloat16)
    in_vmem = pl.BlockSpec(memory_space=pltpu.VMEM)
    in_smem = pl.BlockSpec(memory_space=pltpu.SMEM)
    outgoing, meta = pl.pallas_call(
        functools.partial(plan_kernel, slot_count),
        in_specs=[in_smem, in_smem, in_vmem],
        out_specs=[in_vmem, in_smem],
        out_shape=[slot_shape, jax.ShapeDtypeStruct((3, slot_count), jnp.int32)],
        scratch_shapes=[stage_shape, pltpu.SMEM((loaders,), jnp.int32)],
        compiler_params=pltpu.CompilerParams(vmem_limit_bytes=VMEM_LIMIT),
        name="plan",
    )(lengths, owners, upstream)

    def exchange(slots):
        slots = slots.reshape(loaders, pair_count, span, width)
        moved = lax.all_to_all(slots, "bucket", split_axis=0, concat_axis=0, tiled=True)
        return moved.reshape(slot_count, span, width)

    incoming = exchange(outgoing)

    group = 4
    steps = slot_count // group
    rows = group * span
    row_block = pl.BlockSpec((rows, width), lambda i, *_: (i, 0))
    all_rows = slot_count * span
    gain_row, bn_gain_row, bn_bias_row = ln_gain[None], bn_gain[None], bn_bias[None]
    w_taps = jnp.pad(w_dw.T, ((0, 1), (0, 0)))
    sums_shape = (2 * blocks, LANES)
    params = pltpu.CompilerParams(
        dimension_semantics=("arbitrary",), vmem_limit_bytes=VMEM_LIMIT
    )
    padded_shape = pltpu.VMEM((group, blocks, span, LANES), jnp.float32)

    thin_block = pl.BlockSpec((rows, LANES), lambda i, *_: (i, 0))
    tall = pltpu.HBM((all_rows, width), jnp.float32)
    conv, part, normed, inverse, linear, gate = pl.pallas_call(
        functools.partial(forward_kernel, group, span, taps),
        grid_spec=pltpu.PrefetchScalarGridSpec(
            num_scalar_prefetch=1,
            grid=(steps,),
            in_specs=[row_block, whole((1, width)), whole(w_in.shape), whole(w_taps.shape)],
            out_specs=[
                row_block, whole(sums_shape), row_block, thin_block, row_block, row_block
            ],
            scratch_shapes=[padded_shape],
        ),
        out_shape=[
            tall,
            jax.ShapeDtypeStruct(sums_shape, jnp.float32),
            tall,
            pltpu.HBM((all_rows, LANES), jnp.float32),
            tall,
            tall,
        ],
        compiler_params=params,
        cost_estimate=pl.CostEstimate(
            flops=2 * 10**9, bytes_accessed=4 * 10**7, transcendentals=0
        ),
        name="forward",
    )(meta, frames, gain_row, w_in, w_taps)
    totals = sum_everywhere(part, 0)

    out_rows, grad_bn, back_part, grad_wout = pl.pallas_call(
        functools.partial(middle_kernel, group, span, total_frames),
        grid_spec=pltpu.PrefetchScalarGridSpec(
            num_scalar_prefetch=1,
            grid=(steps,),
            in_specs=[
                row_block, whole(slot_shape.shape), whole(sums_shape), whole((1, width)),
                whole((1, width)), whole(w_out.shape),
            ],
            out_specs=[whole(slot_shape.shape), row_block, whole(sums_shape), whole(w_out.shape)],
        ),
        out_shape=[
            slot_shape,
            tall,
            jax.ShapeDtypeStruct(sums_shape, jnp.float32),
            pltpu.HBM(w_out.shape, jnp.float32),
        ],
        compiler_params=params,
        cost_estimate=pl.CostEstimate(
            flops=3 * 10**9, bytes_accessed=2 * 10**7, transcendentals=0
        ),
        name="middle",
    )(meta, in_hbm(conv), incoming, totals, bn_gain_row, bn_bias_row, w_out)

    back_totals = sum_everywhere(back_part, 1)
    leaving, back_totals = lax.optimization_barrier((out_rows, back_totals))
    arrived = exchange(leaving)

    share = width // loaders
    packed_rows = (w_in.shape[1] // LANES + blocks + 1) * share
    grad_frames, packed = pl.pallas_call(
        functools.partial(backward_kernel, group, span, taps, total_frames),
        grid_spec=pltpu.PrefetchScalarGridSpec(
            num_scalar_prefetch=1,
            grid=(steps,),
            in_specs=[
                row_block, thin_block, row_block, row_block, row_block, row_block,
                whole(sums_shape), whole(sums_shape),
                whole((1, width)), whole((1, width)), whole(w_in.shape), whole(w_taps.shape),
                whole(w_out.shape),
            ],
            out_specs=[row_block, whole((loaders, packed_rows, LANES))],
            scratch_shapes=[
                padded_shape,
                padded_shape,
                pltpu.VMEM((rows, width), jnp.float32),
                pltpu.VMEM((blocks, taps + 1, SUB, LANES), jnp.float32),
                pltpu.VMEM(w_in.shape, jnp.float32),
                pltpu.VMEM((1, width), jnp.float32),
                pltpu.VMEM((LANES, LANES), jnp.float32),
            ],
        ),
        out_shape=[
            jax.ShapeDtypeStruct((all_rows, width), jnp.bfloat16),
            jax.ShapeDtypeStruct((loaders, packed_rows, LANES), jnp.bfloat16),
        ],
        compiler_params=params,
        cost_estimate=pl.CostEstimate(
            flops=6 * 10**9, bytes_accessed=8 * 10**7, transcendentals=0
        ),
        name="backward",
    )(
        meta, *map(in_hbm, (normed, inverse, linear, gate, conv, grad_bn)), totals, back_totals, gain_row, bn_gain_row, w_in, w_taps,
        in_hbm(grad_wout),
    )
    reduced = reduce_rows(packed, 2).reshape(-1, share, LANES)
    out_frames, grad_win, grad_wo, last = pl.pallas_call(
        finish_kernel,
        in_specs=[in_smem, in_vmem, in_vmem],
        out_specs=[in_vmem] * 4,
        out_shape=[
            jax.ShapeDtypeStruct((own_rows, width), jnp.bfloat16),
            jax.ShapeDtypeStruct((share, w_in.shape[1]), jnp.float32),
            jax.ShapeDtypeStruct((share, width), jnp.float32),
            jax.ShapeDtypeStruct((share, LANES), jnp.float32),
        ],
        scratch_shapes=[stage_shape],
        compiler_params=pltpu.CompilerParams(vmem_limit_bytes=VMEM_LIMIT),
        name="finish",
    )(meta, arrived, reduced)
    flat_back = back_totals.reshape(2, width)
    return (
        out_frames,
        grad_frames,
        grad_win,
        grad_wo,
        last[:, :taps],
        last[:, taps],
        flat_back[1],
        flat_back[0],
    )


def solution(mesh):
    placed = (
        P(("dp", "bucket"), None),
        P("dp", None),
        P("dp", None),
        P(("dp", "bucket"), None),
        P(),
        P(),
        P(),
        P(),
        P(),
        P(),
    )
    return jax.shard_map(
        local,
        mesh=mesh,
        in_specs=placed,
        out_specs=(
            P(("dp", "bucket"), None),
            P(("dp", "bucket"), None),
            P("bucket", None),
            P("bucket", None),
            P("bucket", None),
            P("bucket"),
            P(),
            P(),
        ),
        check_vma=False,
    )
```

```python
import functools

import jax
import jax.numpy as jnp
from jax import lax
from jax.experimental import pallas as pl
from jax.experimental.pallas import tpu as pltpu
from jax.sharding import PartitionSpec as P

EPSILON = 1e-05
LANES = 128
SUB = 8
MESH = pl.DeviceIdType.MESH
VMEM_LIMIT = 24 << 20


def lane(c):
    return slice(c * LANES, (c + 1) * LANES)


def row_of(packed, first, blocks):
    return jnp.concatenate([packed[first + c : first + c + 1] for c in range(blocks)], axis=1)


def live_rows(lens_ref, first, count, span, width):
    position = lax.broadcasted_iota(jnp.int32, (span, width), 0)
    return [position < lens_ref[0, first + i] for i in range(count)]


def keep_live(values, masks, span):
    parts = [
        jnp.where(masks[i], values[i * span : (i + 1) * span], 0.0) for i in range(len(masks))
    ]
    return jnp.concatenate(parts, axis=0)


def layer_norm(frame_rows):
    values = frame_rows.astype(jnp.float32)
    centred = values - jnp.mean(values, axis=1, keepdims=True)
    inverse = lax.rsqrt(jnp.mean(centred * centred, axis=1, keepdims=True) + EPSILON)
    return centred * inverse, inverse


def project(frame_rows, gain, w_in):
    normed, inverse = layer_norm(frame_rows)
    h = (normed * gain).astype(jnp.bfloat16)
    projected = jnp.dot(h, w_in, preferred_element_type=jnp.float32)
    half = projected.shape[1] // 2
    return normed, inverse, projected[:, :half], jax.nn.sigmoid(projected[:, half:])


def shifted_sum(frame, weight, span, taps):
    lead = (taps + 1) // 2 // SUB
    count = span // SUB
    tiles = [frame[i * SUB : (i + 1) * SUB] for i in range(count)]
    total = None
    for residue in range(SUB):
        shifts = [k for k in range(residue, taps + 1, SUB) if k > 0]
        weights = {k: jnp.broadcast_to(weight(k), (SUB, LANES)) for k in shifts}
        parts = []
        for i in range(count + 1 if residue else count):
            part = None
            for k in shifts:
                at = (k - residue) // SUB + i - lead
                if 0 <= at < count:
                    term = tiles[at] * weights[k]
                    part = term if part is None else part + term
            parts.append(jnp.zeros((SUB, LANES), jnp.float32) if part is None else part)
        moved = jnp.concatenate(parts, axis=0)
        if residue:
            moved = pltpu.roll(moved, span + SUB - residue, 0)[:span]
        total = moved if total is None else total + moved
    return total


def forward_kernel(group, span, taps, lens_ref, frames_ref, gain_ref, w_in_ref, w_dw_ref,
                   conv_ref, sums_ref, normed_ref, inverse_ref, linear_ref, gate_ref, padded):
    step = pl.program_id(0)
    blocks = conv_ref.shape[1] // LANES

    @pl.when(step == 0)
    def _():
        sums_ref[...] = jnp.zeros_like(sums_ref)

    masks = live_rows(lens_ref, step * group, group, span, conv_ref.shape[1])
    normed, inverse, linear, gate = project(frames_ref[...], gain_ref[...], w_in_ref[...])
    normed_ref[...] = normed
    inverse_ref[...] = jnp.broadcast_to(inverse, inverse_ref.shape)
    linear_ref[...] = linear
    gate_ref[...] = gate
    gated = keep_live(linear * gate, masks, span).astype(jnp.bfloat16).astype(jnp.float32)
    for u in range(group):
        for c in range(blocks):
            padded[u, c] = gated[u * span : (u + 1) * span, lane(c)]

    def one(u, carry):
        live = lax.broadcasted_iota(jnp.int32, (span, LANES), 0) < lens_ref[0, step * group + u]
        start = pl.multiple_of(u * span, SUB)
        for c in range(blocks):
            conv = shifted_sum(
                padded[u, c], lambda k: w_dw_ref[k - 1 : k, lane(c)], span, taps
            )
            conv_ref[pl.ds(start, span), lane(c)] = conv
            masked = jnp.where(live, conv, 0.0)
            sums_ref[c : c + 1] += jnp.sum(masked, axis=0, keepdims=True)
            sums_ref[blocks + c : blocks + c + 1] += jnp.sum(
                masked * masked, axis=0, keepdims=True
            )
        return carry

    lax.fori_loop(0, group, one, 0)


def batch_norm(total_ref, conv, total_frames, blocks):
    packed = total_ref[...]
    centre = row_of(packed, 0, blocks) / total_frames
    variance = row_of(packed, blocks, blocks) / total_frames - centre * centre
    inverse = lax.rsqrt(variance + EPSILON)
    return (conv - centre) * inverse, inverse


def middle_kernel(group, span, total_frames, lens_ref, conv_ref, dy_ref, total_ref, bn_gain_ref,
                  bn_bias_ref, w_out_ref, out_ref, grad_bn_ref, sums_ref, grad_wout_ref):
    step = pl.program_id(0)
    width = conv_ref.shape[1]
    blocks = width // LANES

    @pl.when(step == 0)
    def _():
        sums_ref[...] = jnp.zeros_like(sums_ref)
        grad_wout_ref[...] = jnp.zeros_like(grad_wout_ref)

    masks = live_rows(lens_ref, step * group, group, span, width)
    slots = [lens_ref[1, step * group + i] for i in range(group)]
    arrived = jnp.concatenate([dy_ref[slot] for slot in slots], axis=0)
    dy = keep_live(arrived.astype(jnp.float32), masks, span).astype(jnp.bfloat16)
    w_out = w_out_ref[...]
    bn_normed, _ = batch_norm(total_ref, conv_ref[...], total_frames, blocks)
    bn = bn_normed * bn_gain_ref[...] + bn_bias_ref[...]
    sig = jax.nn.sigmoid(bn)
    swished = (bn * sig).astype(jnp.bfloat16)
    out = jnp.dot(swished, w_out, preferred_element_type=jnp.float32).astype(jnp.bfloat16)
    for i in range(group):
        out_ref[slots[i]] = out[i * span : (i + 1) * span]
    grad_wout_ref[...] += lax.dot_general(
        swished, dy, (((0,), (0,)), ((), ())), preferred_element_type=jnp.float32
    )
    grad_swish = lax.dot_general(
        dy, w_out, (((1,), (1,)), ((), ())), preferred_element_type=jnp.float32
    )
    grad_bn = grad_swish * (sig * (1.0 + bn * (1.0 - sig)))
    grad_bn_ref[...] = grad_bn
    bias_row = jnp.sum(grad_bn, axis=0, keepdims=True)
    gain_row = jnp.sum(grad_bn * bn_normed, axis=0, keepdims=True)
    for c in range(blocks):
        sums_ref[c : c + 1] += bias_row[:, lane(c)]
        sums_ref[blocks + c : blocks + c + 1] += gain_row[:, lane(c)]


def backward_kernel(group, span, taps, total_frames, lens_ref, normed_ref, inverse_ref,
                    linear_ref, gate_ref, conv_ref, grad_bn_ref,
                    total_ref, back_ref, gain_ref, bn_gain_ref, w_in_ref, w_dw_ref, wout_ref,
                    grad_frames_ref, packed_ref, padded, grad_pad, gated_grad, w_acc, win_acc,
                    ln_acc, flat):
    step = pl.program_id(0)
    width = conv_ref.shape[1]
    blocks = width // LANES
    count = span // SUB
    lead = (taps + 1) // 2 // SUB

    @pl.when(step == 0)
    def _():
        w_acc[...] = jnp.zeros_like(w_acc)
        win_acc[...] = jnp.zeros_like(win_acc)
        ln_acc[...] = jnp.zeros_like(ln_acc)

    masks = live_rows(lens_ref, step * group, group, span, width)
    w_in = w_in_ref[...]
    gated = keep_live(linear_ref[...] * gate_ref[...], masks, span).astype(jnp.bfloat16).astype(jnp.float32)
    bn_normed, bn_inverse = batch_norm(total_ref, conv_ref[...], total_frames, blocks)
    back = back_ref[...]
    bias_mean = row_of(back, 0, blocks) / total_frames
    gain_mean = row_of(back, blocks, blocks) / total_frames
    grad_conv = keep_live(
        bn_gain_ref[...] * bn_inverse * (grad_bn_ref[...] - bias_mean - bn_normed * gain_mean),
        masks,
        span,
    )
    for u in range(group):
        for c in range(blocks):
            rows = slice(u * span, (u + 1) * span)
            padded[u, c] = gated[rows, lane(c)]
            grad_pad[u, c] = grad_conv[rows, lane(c)]

    def one(u, carry):
        start = pl.multiple_of(u * span, SUB)
        for c in range(blocks):
            grads = grad_pad[u, c]
            gated_grad[pl.ds(start, span), lane(c)] = shifted_sum(
                grads, lambda k: w_dw_ref[taps - k : taps - k + 1, lane(c)], span, taps
            )
            blank = jnp.zeros((SUB, LANES), jnp.float32)
            inner = jnp.concatenate([blank, grads, blank], axis=0)
            frame = padded[u, c]
            for residue in range(SUB):
                moved = inner if residue == 0 else pltpu.roll(inner, residue, 0)
                moved = moved[SUB:]
                for k in range(residue, taps + 1, SUB):
                    if k == 0:
                        continue
                    part = None
                    for i in range(count + 1 if residue else count):
                        at = (k - residue) // SUB + i - lead
                        if 0 <= at < count:
                            tile = frame[at * SUB : (at + 1) * SUB]
                            term = moved[i * SUB : (i + 1) * SUB] * tile
                            part = term if part is None else part + term
                    w_acc[c, k - 1] += part
        return carry

    lax.fori_loop(0, group, one, 0)

    grad_gated = keep_live(gated_grad[...], masks, span)
    linear, gate = linear_ref[...], gate_ref[...]
    normed, inverse = normed_ref[...], inverse_ref[:, :1]
    h = (normed * gain_ref[...]).astype(jnp.bfloat16)
    left = grad_gated * gate
    grad_a = jnp.concatenate(
        [left.astype(jnp.bfloat16), (left * linear * (1.0 - gate)).astype(jnp.bfloat16)], axis=1
    )
    win_acc[...] += lax.dot_general(
        h, grad_a, (((0,), (0,)), ((), ())), preferred_element_type=jnp.float32
    )
    grad_h = lax.dot_general(
        grad_a, w_in, (((1,), (1,)), ((), ())), preferred_element_type=jnp.float32
    )
    ln_acc[...] += jnp.sum(grad_h * normed, axis=0, keepdims=True)
    scaled = grad_h * gain_ref[...]
    inner_mean = jnp.mean(scaled * normed, axis=1, keepdims=True)
    grad_x = inverse * (scaled - jnp.mean(scaled, axis=1, keepdims=True) - normed * inner_mean)
    grad_frames_ref[...] = keep_live(grad_x, masks, span).astype(jnp.bfloat16)

    @pl.when(step == pl.num_programs(0) - 1)
    def _():
        owners = packed_ref.shape[0]
        share = width // owners
        wide = w_in.shape[1] // LANES
        for c in range(blocks):
            flat[...] = jnp.zeros_like(flat)
            for k in range(taps):
                flat[k : k + 1] = jnp.sum(w_acc[c, k], axis=0, keepdims=True)
            flat[taps : taps + 1] = ln_acc[:, lane(c)]
            turned = flat[...].T.astype(jnp.bfloat16)
            for i in range(LANES // share):
                packed_ref[c * (LANES // share) + i, (wide + blocks) * share :] = turned[
                    i * share : (i + 1) * share
                ]
        for j in range(owners):
            rows = slice(j * share, (j + 1) * share)
            for c in range(wide):
                packed_ref[j, c * share : (c + 1) * share] = win_acc[rows, lane(c)].astype(
                    jnp.bfloat16
                )
            for c in range(blocks):
                packed_ref[j, (wide + c) * share : (wide + c + 1) * share] = wout_ref[
                    rows, lane(c)
                ].astype(jnp.bfloat16)


def plan_kernel(slots, lens_ref, owners_ref, up_ref, out_ref, meta_ref, stage, counts, begin):
    me = lax.axis_index("bucket")
    own_rows, width = up_ref.shape
    span = out_ref.shape[1]
    blocks = width // LANES
    loaders = lens_ref.shape[1] // slots
    pairs = slots // loaders
    for c in range(blocks):
        stage[c, :own_rows] = up_ref[:, lane(c)].astype(jnp.float32)
        stage[c, own_rows:] = jnp.zeros((span, LANES), jnp.float32)

    def look(i, carry):
        found, start = carry
        for j in range(SUB):
            at = i * SUB + j
            mine = owners_ref[0, at] == me
            begin[found] = start
            found = found + jnp.where(mine, 1, 0)
            start = start + jnp.where(mine, lens_ref[0, at], 0)
        return found, start

    lax.fori_loop(0, loaders * slots // SUB, look, (jnp.int32(0), jnp.int32(0)))

    def move(i, carry):
        start = begin[i]
        meta_ref[2, i] = start
        for c in range(blocks):
            out_ref[i, :, lane(c)] = stage[c, pl.ds(start, span)].astype(jnp.bfloat16)
        return carry

    lax.fori_loop(0, slots, move, 0)

    def clear(i, carry):
        counts[i] = 0
        return carry

    lax.fori_loop(0, loaders, clear, 0)

    def place(i, carry):
        owner = owners_ref[0, me * slots + i]
        rank = counts[owner]
        counts[owner] = rank + 1
        meta_ref[0, i] = lens_ref[0, me * slots + i]
        meta_ref[1, i] = owner * pairs + rank
        return carry

    lax.fori_loop(0, slots, place, 0)


def finish_kernel(meta_ref, arrived_ref, reduced_ref, out_ref, win_ref, wout_ref, last_ref, stage):
    slots, span, width = arrived_ref.shape
    own_rows = out_ref.shape[0]
    blocks = width // LANES
    wide = win_ref.shape[1] // LANES

    def place(u, carry):
        start = meta_ref[2, u]
        for c in range(blocks):
            stage[c, pl.ds(start, span)] = arrived_ref[u, :, lane(c)].astype(jnp.float32)
        return carry

    lax.fori_loop(0, slots, place, 0)
    for c in range(blocks):
        out_ref[:, lane(c)] = stage[c, :own_rows].astype(jnp.bfloat16)
        wout_ref[:, lane(c)] = reduced_ref[wide + c].astype(jnp.float32)
    for c in range(wide):
        win_ref[:, lane(c)] = reduced_ref[c].astype(jnp.float32)
    last_ref[...] = reduced_ref[wide + blocks].astype(jnp.float32)


def whole(shape):
    return pl.BlockSpec(shape, lambda i, *_: (0,) * len(shape))


def sum_kernel(groups, owners, part_ref, out_ref, slots, send_sems, recv_sems):
    count = groups * owners
    me = lax.axis_index("dp") * owners + lax.axis_index("bucket")
    barrier = pltpu.get_barrier_semaphore()

    def peer_of(i):
        other = lax.rem(me + i, count)
        return (other // owners, lax.rem(other, owners))

    def greet(i, carry):
        pl.semaphore_signal(barrier, inc=1, device_id=peer_of(i), device_id_type=MESH)
        return carry

    lax.fori_loop(1, count, greet, 0)
    pl.semaphore_wait(barrier, count - 1)

    def copy_to(i):
        return pltpu.make_async_remote_copy(
            src_ref=part_ref,
            dst_ref=slots.at[me],
            send_sem=send_sems.at[i],
            recv_sem=recv_sems.at[me],
            device_id=peer_of(i),
            device_id_type=MESH,
        )

    def send(i, carry):
        copy_to(i).start()
        return carry

    lax.fori_loop(1, count, send, 0)
    slots[me] = part_ref[...]

    def receive(i, carry):
        source = lax.rem(me + i, count)
        pltpu.make_async_remote_copy(
            src_ref=part_ref,
            dst_ref=slots.at[source],
            send_sem=send_sems.at[i],
            recv_sem=recv_sems.at[source],
            device_id=peer_of(i),
            device_id_type=MESH,
        ).wait_recv()
        return carry

    lax.fori_loop(1, count, receive, 0)
    out_ref[...] = lax.fori_loop(
        1, count, lambda i, total: total + slots[i], slots[0]
    )

    def sent(i, carry):
        copy_to(i).wait_send()
        return carry

    lax.fori_loop(1, count, sent, 0)


def sum_everywhere(part, collective_id):
    groups, owners = lax.axis_size("dp"), lax.axis_size("bucket")
    count = groups * owners
    return pl.pallas_call(
        functools.partial(sum_kernel, groups, owners),
        out_shape=jax.ShapeDtypeStruct(part.shape, part.dtype),
        in_specs=[pl.BlockSpec(memory_space=pltpu.VMEM)],
        out_specs=pl.BlockSpec(memory_space=pltpu.VMEM),
        scratch_shapes=[
            pltpu.VMEM((count,) + part.shape, part.dtype),
            pltpu.SemaphoreType.DMA((count,)),
            pltpu.SemaphoreType.DMA((count,)),
        ],
        compiler_params=pltpu.CompilerParams(
            collective_id=collective_id, has_side_effects=True, vmem_limit_bytes=4 << 20
        ),
        cost_estimate=pl.CostEstimate(flops=10**6, bytes_accessed=2 * 10**7, transcendentals=0),
        name="sum_everywhere_%d" % collective_id,
    )(part)


def reduce_kernel(groups, owners, src, out, first, first_sum, second, second_sum, third, mine,
                  core_sems, pair_sems, row_sems, all_sems):
    dp, me = lax.axis_index("dp"), lax.axis_index("bucket")
    halves = groups // 2
    core, side = lax.rem(dp, 2), dp // 2
    chunk = core * halves + side
    partner = side * 2 + (1 - core)
    barrier = pltpu.get_barrier_semaphore()

    def group_peer(i):
        return lax.rem(dp + i, groups)

    def owner_peer(i):
        return lax.rem(me + i, owners)

    def greet_group(i, carry):
        pl.semaphore_signal(barrier, inc=1, device_id=(group_peer(i), me), device_id_type=MESH)
        return carry

    def greet_owner(i, carry):
        pl.semaphore_signal(barrier, inc=1, device_id=(dp, owner_peer(i)), device_id_type=MESH)
        return carry

    lax.fori_loop(1, groups, greet_group, 0)
    lax.fori_loop(1, owners, greet_owner, 0)
    pl.semaphore_wait(barrier, groups + owners - 2)

    def remote(source, target, sems, i, j, device):
        return pltpu.make_async_remote_copy(
            src_ref=source,
            dst_ref=target,
            send_sem=sems.at[0, i],
            recv_sem=sems.at[1, j],
            device_id=device,
            device_id_type=MESH,
        )

    def bucket_of(i):
        return lax.rem(me + 1 + i, owners)

    def swap(i):
        bucket = bucket_of(i)
        return remote(src.at[bucket, 1 - core], first.at[bucket], core_sems, i, i, (partner, me))

    def to_side(i, n, arriving):
        bucket = bucket_of(i)
        other = lax.rem(side + n, halves)
        slot = other if arriving else side
        return remote(
            first_sum.at[bucket, other], second.at[slot, bucket], pair_sems,
            n * owners + i, slot * owners + i, (other * 2 + core, me),
        )

    def to_owner(i, arriving):
        other = owner_peer(i)
        slot = other if arriving else me
        return remote(second_sum.at[other], third.at[slot], row_sems, i, slot, (dp, other))

    def start_swap(i, carry):
        swap(i).start()
        return carry

    def add_first(i, carry):
        bucket = bucket_of(i)
        swap(i).wait_recv()
        total = src[bucket, core].astype(jnp.float32) + first[bucket].astype(jnp.float32)
        first_sum[bucket] = total.astype(jnp.bfloat16)
        for n in range(1, halves):
            to_side(i, n, False).start()
        return carry

    def add_second(i, carry):
        bucket = bucket_of(i)
        total = first_sum[bucket, side].astype(jnp.float32)
        for n in range(1, halves):
            to_side(i, n, True).wait_recv()
            total = total + second[lax.rem(side + n, halves), bucket].astype(jnp.float32)
        second_sum[bucket] = total.astype(jnp.bfloat16)
        return carry

    def add_and_send(i, carry):
        add_second(i, carry)
        to_owner(i + 1, False).start()
        return carry

    def wait_owner(i, carry):
        to_owner(i, True).wait_recv()
        return carry

    lax.fori_loop(0, owners, start_swap, 0)
    lax.fori_loop(0, owners, add_first, 0)
    lax.fori_loop(0, owners - 1, add_and_send, 0)
    add_second(owners - 1, 0)
    third[me] = second_sum[me]
    lax.fori_loop(1, owners, wait_owner, 0)
    total = lax.fori_loop(
        1, owners, lambda i, t: t + third[i].astype(jnp.float32), third[0].astype(jnp.float32)
    )
    mine[...] = total.astype(jnp.bfloat16)

    def to_group(i, arriving):
        other = group_peer(i)
        device = other if arriving else dp
        slot = lax.rem(device, 2) * halves + device // 2
        return remote(mine, out.at[slot], all_sems, i, slot, (other, me))

    def send_group(i, carry):
        to_group(i, False).start()
        return carry

    def wait_group(i, carry):
        to_group(i, True).wait_recv()
        return carry

    lax.fori_loop(1, groups, send_group, 0)
    out[chunk] = mine[...]
    lax.fori_loop(1, groups, wait_group, 0)

    def sent_owner(i, carry):
        to_owner(i, False).wait_send()
        return carry

    def sent_group(i, carry):
        to_group(i, False).wait_send()
        return carry

    def sent_first(i, carry):
        swap(i).wait_send()
        for n in range(1, halves):
            to_side(i, n, False).wait_send()
        return carry

    lax.fori_loop(0, owners, sent_first, 0)
    lax.fori_loop(1, owners, sent_owner, 0)
    lax.fori_loop(1, groups, sent_group, 0)


def reduce_rows(packed, collective_id):
    groups, owners = lax.axis_size("dp"), lax.axis_size("bucket")
    halves = groups // 2
    rows = packed.shape[1] // groups
    source = packed.reshape(owners, 2, halves, rows, LANES)
    kind = jnp.bfloat16
    return pl.pallas_call(
        functools.partial(reduce_kernel, groups, owners),
        out_shape=jax.ShapeDtypeStruct((groups, rows, LANES), kind),
        in_specs=[pl.BlockSpec(memory_space=pltpu.VMEM)],
        out_specs=pl.BlockSpec(memory_space=pltpu.VMEM),
        scratch_shapes=[
            pltpu.VMEM((owners, halves, rows, LANES), kind),
            pltpu.VMEM((owners, halves, rows, LANES), kind),
            pltpu.VMEM((halves, owners, rows, LANES), kind),
            pltpu.VMEM((owners, rows, LANES), kind),
            pltpu.VMEM((owners, rows, LANES), kind),
            pltpu.VMEM((rows, LANES), kind),
            pltpu.SemaphoreType.DMA((2, owners)),
            pltpu.SemaphoreType.DMA((2, halves * owners)),
            pltpu.SemaphoreType.DMA((2, owners)),
            pltpu.SemaphoreType.DMA((2, groups)),
        ],
        compiler_params=pltpu.CompilerParams(
            collective_id=collective_id, has_side_effects=True, vmem_limit_bytes=16 << 20
        ),
        cost_estimate=pl.CostEstimate(flops=10**7, bytes_accessed=6 * 10**7, transcendentals=0),
        name="reduce_rows",
    )(source)


def in_hbm(array):
    return pltpu.with_memory_space_constraint(array, pltpu.HBM)


def local(frames, lengths, owners, upstream, ln_gain, w_in, w_dw, bn_gain, bn_bias, w_out):
    loaders = lax.axis_size("bucket")
    width = frames.shape[1]
    taps = w_dw.shape[1]
    slot_count = lengths.shape[1] // loaders
    span = frames.shape[0] // slot_count
    pair_count = slot_count // loaders
    own_rows = upstream.shape[0]
    blocks = width // LANES
    total_frames = float(own_rows * loaders * lax.axis_size("dp"))
    stage_shape = pltpu.VMEM((blocks, own_rows + span, LANES), jnp.float32)
    slot_shape = jax.ShapeDtypeStruct((slot_count, span, width), jnp.bfloat16)
    in_vmem = pl.BlockSpec(memory_space=pltpu.VMEM)
    in_smem = pl.BlockSpec(memory_space=pltpu.SMEM)
    outgoing, meta = pl.pallas_call(
        functools.partial(plan_kernel, slot_count),
        in_specs=[in_smem, in_smem, in_vmem],
        out_specs=[in_vmem, in_smem],
        out_shape=[slot_shape, jax.ShapeDtypeStruct((3, slot_count), jnp.int32)],
        scratch_shapes=[
            stage_shape,
            pltpu.SMEM((loaders,), jnp.int32),
            pltpu.SMEM((slot_count + 1,), jnp.int32),
        ],
        compiler_params=pltpu.CompilerParams(vmem_limit_bytes=VMEM_LIMIT),
        name="plan",
    )(in_hbm(lengths), in_hbm(owners), in_hbm(upstream))

    def exchange(slots):
        slots = slots.reshape(loaders, pair_count, span, width)
        moved = lax.all_to_all(slots, "bucket", split_axis=0, concat_axis=0, tiled=True)
        return moved.reshape(slot_count, span, width)

    incoming = exchange(outgoing)

    group = 4
    steps = slot_count // group
    rows = group * span
    row_block = pl.BlockSpec((rows, width), lambda i, *_: (i, 0))
    all_rows = slot_count * span
    gain_row, bn_gain_row, bn_bias_row = ln_gain[None], bn_gain[None], bn_bias[None]
    w_taps = jnp.pad(w_dw.T, ((0, 1), (0, 0)))
    sums_shape = (2 * blocks, LANES)
    params = pltpu.CompilerParams(
        dimension_semantics=("arbitrary",), vmem_limit_bytes=VMEM_LIMIT
    )
    padded_shape = pltpu.VMEM((group, blocks, span, LANES), jnp.float32)

    thin_block = pl.BlockSpec((rows, LANES), lambda i, *_: (i, 0))
    tall = pltpu.HBM((all_rows, width), jnp.float32)
    conv, part, normed, inverse, linear, gate = pl.pallas_call(
        functools.partial(forward_kernel, group, span, taps),
        grid_spec=pltpu.PrefetchScalarGridSpec(
            num_scalar_prefetch=1,
            grid=(steps,),
            in_specs=[row_block, whole((1, width)), whole(w_in.shape), whole(w_taps.shape)],
            out_specs=[
                row_block, whole(sums_shape), row_block, thin_block, row_block, row_block
            ],
            scratch_shapes=[padded_shape],
        ),
        out_shape=[
            tall,
            jax.ShapeDtypeStruct(sums_shape, jnp.float32),
            tall,
            pltpu.HBM((all_rows, LANES), jnp.float32),
            tall,
            tall,
        ],
        compiler_params=params,
        cost_estimate=pl.CostEstimate(
            flops=2 * 10**9, bytes_accessed=4 * 10**7, transcendentals=0
        ),
        name="forward",
    )(meta, frames, gain_row, w_in, w_taps)
    totals = sum_everywhere(part, 0)

    out_rows, grad_bn, back_part, grad_wout = pl.pallas_call(
        functools.partial(middle_kernel, group, span, total_frames),
        grid_spec=pltpu.PrefetchScalarGridSpec(
            num_scalar_prefetch=1,
            grid=(steps,),
            in_specs=[
                row_block, whole(slot_shape.shape), whole(sums_shape), whole((1, width)),
                whole((1, width)), whole(w_out.shape),
            ],
            out_specs=[whole(slot_shape.shape), row_block, whole(sums_shape), whole(w_out.shape)],
        ),
        out_shape=[
            slot_shape,
            tall,
            jax.ShapeDtypeStruct(sums_shape, jnp.float32),
            pltpu.HBM(w_out.shape, jnp.float32),
        ],
        compiler_params=params,
        cost_estimate=pl.CostEstimate(
            flops=3 * 10**9, bytes_accessed=2 * 10**7, transcendentals=0
        ),
        name="middle",
    )(meta, in_hbm(conv), incoming, totals, bn_gain_row, bn_bias_row, w_out)

    back_totals = sum_everywhere(back_part, 1)
    leaving, back_totals = lax.optimization_barrier((out_rows, back_totals))
    arrived = exchange(leaving)

    share = width // loaders
    packed_rows = (w_in.shape[1] // LANES + blocks + 1) * share
    grad_frames, packed = pl.pallas_call(
        functools.partial(backward_kernel, group, span, taps, total_frames),
        grid_spec=pltpu.PrefetchScalarGridSpec(
            num_scalar_prefetch=1,
            grid=(steps,),
            in_specs=[
                row_block, thin_block, row_block, row_block, row_block, row_block,
                whole(sums_shape), whole(sums_shape),
                whole((1, width)), whole((1, width)), whole(w_in.shape), whole(w_taps.shape),
                whole(w_out.shape),
            ],
            out_specs=[row_block, whole((loaders, packed_rows, LANES))],
            scratch_shapes=[
                padded_shape,
                padded_shape,
                pltpu.VMEM((rows, width), jnp.float32),
                pltpu.VMEM((blocks, taps + 1, SUB, LANES), jnp.float32),
                pltpu.VMEM(w_in.shape, jnp.float32),
                pltpu.VMEM((1, width), jnp.float32),
                pltpu.VMEM((LANES, LANES), jnp.float32),
            ],
        ),
        out_shape=[
            jax.ShapeDtypeStruct((all_rows, width), jnp.bfloat16),
            jax.ShapeDtypeStruct((loaders, packed_rows, LANES), jnp.bfloat16),
        ],
        compiler_params=params,
        cost_estimate=pl.CostEstimate(
            flops=6 * 10**9, bytes_accessed=8 * 10**7, transcendentals=0
        ),
        name="backward",
    )(
        meta, *map(in_hbm, (normed, inverse, linear, gate, conv, grad_bn)), totals, back_totals, gain_row, bn_gain_row, w_in, w_taps,
        in_hbm(grad_wout),
    )
    reduced = reduce_rows(packed, 2).reshape(-1, share, LANES)
    out_frames, grad_win, grad_wo, last = pl.pallas_call(
        finish_kernel,
        in_specs=[in_smem, in_vmem, in_vmem],
        out_specs=[in_vmem] * 4,
        out_shape=[
            jax.ShapeDtypeStruct((own_rows, width), jnp.bfloat16),
            jax.ShapeDtypeStruct((share, w_in.shape[1]), jnp.float32),
            jax.ShapeDtypeStruct((share, width), jnp.float32),
            jax.ShapeDtypeStruct((share, LANES), jnp.float32),
        ],
        scratch_shapes=[stage_shape],
        compiler_params=pltpu.CompilerParams(vmem_limit_bytes=VMEM_LIMIT),
        name="finish",
    )(meta, arrived, reduced)
    flat_back = back_totals.reshape(2, width)
    return (
        out_frames,
        grad_frames,
        grad_win,
        grad_wo,
        last[:, :taps],
        last[:, taps],
        flat_back[1],
        flat_back[0],
    )


def solution(mesh):
    placed = (
        P(("dp", "bucket"), None),
        P("dp", None),
        P("dp", None),
        P(("dp", "bucket"), None),
        P(),
        P(),
        P(),
        P(),
        P(),
        P(),
    )
    return jax.shard_map(
        local,
        mesh=mesh,
        in_specs=placed,
        out_specs=(
            P(("dp", "bucket"), None),
            P(("dp", "bucket"), None),
            P("bucket", None),
            P("bucket", None),
            P("bucket", None),
            P("bucket"),
            P(),
            P(),
        ),
        check_vma=False,
    )
```
